256 devices in a mesh: ctx: 64 (over x, y_hi, z), tp: 4 (over y_lo, core).
Axes of the slice: x: 4, y: 4 (y_hi: 2, y_lo: 2; y = y_hi * 2 + y_lo), z: 8, core: 2. Of those that a mesh axis runs over, the one named last changes fastest.
Arguments:
- query_pre: bfloat16 [8192, 4096], P('ctx', 'tp'), may hold values from -6 to 6
- key_pre: bfloat16 [8192, 4096], P('ctx', 'tp'), may hold values from -6 to 6
- value_pre: bfloat16 [8192, 4096], P('ctx', 'tp'), may hold values from -6 to 6
- grad_out: bfloat16 [8192, 4096], P('ctx', 'tp'), may hold values from -6 to 6
- w_value: bfloat16 [4096, 4096], P(None, 'tp'), may hold values from -0.09375 to 0.09375
- short_taps: float32 [4096, 3, 3], P('tp'), may hold values from -3 to 3
- residues: float32 [4096, 16], P('tp'), may hold values from -0.3 to 0.3
- decay_rates: float32 [4096, 16], P('tp'), may hold values from 2.4414062e-06 to 0.05
- skip: float32 [4096], P('tp'), may hold values from -3 to 3
Outputs:
- input_grad: bfloat16 [8192, 4096], P(('ctx', 'tp'))
- query_grad: bfloat16 [8192, 4096], P('ctx', 'tp')
- key_grad: bfloat16 [8192, 4096], P('ctx', 'tp')
- d_residues: float32 [4096, 16], P('tp')
- d_skip: float32 [4096], P('tp')
- d_taps: float32 [4096, 3, 3], P('tp')
The draws below stay inside these ranges and needn't reach their ends.
All inputs are finite; a program needn't handle non-finite values.
Results may differ from the reference program's by a relative error of at most 0.009.
Values may be sent and summed in bfloat16 or wider, within the bound.
A program may use at most 128 MiB of HBM per device.

```python
import math
import jax
import jax.numpy as jnp
from jax import lax

WIDTH = 4096
CHANNELS = 4096
MODES = 16
SHORT = 3
TOKENS = 8192
N_TP = 4


def block_scale(stream_key, dims, split, smallest, high):
    factor_of, own = 1.0, jax.random.fold_in(stream_key, 6)
    for position, shards_of in split:
        steps = jnp.exp(jax.random.uniform(jax.random.fold_in(own, position), (shards_of,), jnp.float32, smallest / len(split), high / len(split)))
        factor_of = factor_of * jnp.repeat(steps, dims[position] // shards_of).reshape([-1 if axis == position else 1 for axis in range(len(dims))])
    return factor_of


def normal_values(key, extent, spread, most, split=(), held_as=jnp.bfloat16):
    array = spread * jax.random.normal(key, extent, jnp.float32)
    if split:
        array = array * block_scale(key, extent, split, -0.22, 0.18)
    return jnp.clip(array, -most, most).astype(held_as)


def setup_inputs(seed: int = 0) -> dict:
    seeds = jax.random.split(jax.random.key(seed), 10)
    query_pre = normal_values(seeds[0], (TOKENS, CHANNELS), 1.0, 6.0, ((0, 64), (1, 4)))
    key_pre = normal_values(seeds[1], (TOKENS, CHANNELS), 1.0, 6.0, ((0, 64), (1, 4)))
    value_pre = normal_values(seeds[2], (TOKENS, CHANNELS), 1.0, 6.0, ((0, 64), (1, 4)))
    grad_out = normal_values(seeds[3], (TOKENS, CHANNELS), 1.0, 6.0, ((0, 64), (1, 4)))
    w_value = normal_values(seeds[4], (WIDTH, CHANNELS), CHANNELS ** -0.5, 0.09375, ((1, 4),))
    short_taps = normal_values(seeds[5], (CHANNELS, 3, SHORT), 0.5, 3.0, ((0, 4),), jnp.float32)
    residues = normal_values(seeds[6], (CHANNELS, MODES), 0.05, 0.3, ((0, 4),), jnp.float32)
    decay_rates = jnp.clip(jnp.exp(math.log(0.05) - 9.927204 * jax.random.uniform(seeds[7], (CHANNELS, MODES), jnp.float32) ** block_scale(seeds[7], (CHANNELS, MODES), ((0, 4),), -0.2, 0.2)), 2.441406195430318e-06, 0.05)
    skip = normal_values(seeds[8], (CHANNELS,), 0.5, 3.0, ((0, 4),), jnp.float32)
    return {"query_pre": query_pre, "key_pre": key_pre, "value_pre": value_pre, "grad_out": grad_out, "w_value": w_value, "short_taps": short_taps, "residues": residues, "decay_rates": decay_rates, "skip": skip}


def reference(query_pre, key_pre, value_pre, grad_out, w_value, short_taps, residues, decay_rates, skip):
    length = query_pre.shape[0]
    channels = query_pre.shape[1]
    group_size = min(64, channels)
    group_count = channels // group_size
    fft_size = 2 * length
    positions = jnp.arange(length).astype(jnp.float32)

    def regroup(values_in):
        return values_in.astype(jnp.float32).T.reshape(group_count, group_size, length)

    def delayed(values_in, amount):
        return jnp.pad(values_in, ((0, 0), (0, 0), (amount, 0)))[..., :length]

    def advance(values_in, amount):
        return jnp.pad(values_in, ((0, 0), (0, 0), (0, amount)))[..., amount:]

    def one_block(packed):
        stream, cotangent, tap_block, residue_block, rate_block, skip_block = packed
        features = jnp.zeros_like(stream)
        for tap_index in range(SHORT):
            features = features + tap_block[..., tap_index:tap_index + 1] * delayed(stream, tap_index)
        query_feat, key_feat, value_feat = features[0], features[1], features[2]
        mixed_input = key_feat * value_feat
        powers = jnp.exp(-rate_block[:, :, None] * positions)
        kernel = jnp.sum(residue_block[:, :, None] * powers, axis=1)
        kernel_f = jnp.fft.rfft(kernel, n=fft_size, axis=-1)
        mixed_f = jnp.fft.rfft(mixed_input, n=fft_size, axis=-1)
        conv_out = jnp.fft.irfft(kernel_f * mixed_f, n=fft_size, axis=-1)[:, :length]
        grad_query = cotangent * (conv_out + skip_block[:, None] * mixed_input)
        grad_conv = cotangent * query_feat
        flipped_f = jnp.fft.rfft(grad_conv[:, ::-1], n=fft_size, axis=-1)
        back_conv = jnp.fft.irfft(kernel_f * flipped_f, n=fft_size, axis=-1)[:, :length][:, ::-1]
        grad_mixed = back_conv + skip_block[:, None] * grad_conv
        grad_f = jnp.fft.rfft(grad_conv, n=fft_size, axis=-1)
        correlation = jnp.fft.irfft(grad_f * jnp.conj(mixed_f), n=fft_size, axis=-1)[:, :length]
        grad_residues = jnp.sum(correlation[:, None, :] * powers, axis=2)
        grad_skip = jnp.sum(grad_conv * mixed_input, axis=1)
        stream_grads = jnp.stack([grad_query, grad_mixed * value_feat, grad_mixed * key_feat])
        pre_grads = jnp.zeros_like(stream_grads)
        columns = []
        for tap_index in range(SHORT):
            pre_grads = pre_grads + tap_block[..., tap_index:tap_index + 1] * advance(stream_grads, tap_index)
            columns.append(jnp.sum(stream_grads * delayed(stream, tap_index), axis=-1))
        grad_taps = jnp.stack(columns, axis=-1)
        return pre_grads.astype(jnp.bfloat16), grad_residues, grad_skip, grad_taps

    streams = jnp.stack([regroup(query_pre), regroup(key_pre), regroup(value_pre)], axis=1)
    cotangents = regroup(grad_out)
    tap_blocks = jnp.transpose(short_taps.reshape(group_count, group_size, 3, SHORT), (0, 2, 1, 3))
    residue_blocks = residues.reshape(group_count, group_size, MODES)
    rate_blocks = decay_rates.reshape(group_count, group_size, MODES)
    skip_blocks = skip.reshape(group_count, group_size)
    results = lax.map(one_block, (streams, cotangents, tap_blocks, residue_blocks, rate_blocks, skip_blocks))
    pre_grads = jnp.transpose(results[0], (1, 0, 2, 3)).reshape(3, channels, length)
    query_grad = pre_grads[0].T
    key_grad = pre_grads[1].T
    value_grad = pre_grads[2].T
    shard_chans = channels // N_TP
    total = jnp.zeros((length, w_value.shape[0]), jnp.float32)
    for shard in range(N_TP):
        part_rows = value_grad[:, shard * shard_chans:(shard + 1) * shard_chans].astype(jnp.float32)
        part_cols = w_value[:, shard * shard_chans:(shard + 1) * shard_chans].astype(jnp.float32)
        partial_sum = jnp.dot(part_rows, part_cols.T, precision=lax.Precision.HIGHEST,
                              preferred_element_type=jnp.float32)
        total = total + partial_sum.astype(jnp.bfloat16).astype(jnp.float32)
    input_grad = total.astype(jnp.bfloat16)
    d_residues = results[1].reshape(channels, MODES)
    d_skip = results[2].reshape(channels)
    d_taps = jnp.transpose(results[3], (0, 2, 1, 3)).reshape(channels, 3, SHORT)
    return (input_grad, query_grad, key_grad, d_residues, d_skip, d_taps)
```

```python
import jax
import jax.numpy as jnp
from jax import lax
from jax.sharding import PartitionSpec as P

highest = lax.Precision.HIGHEST


def compose(earlier, later):
    return (earlier[0] * later[0], later[0] * earlier[1] + later[1])


def modal_states(signal, rate_table):
    channels, length = signal.shape
    mode_count = rate_table.shape[1]
    block_len = min(128, length)
    blocks = length // block_len
    offsets = jnp.arange(block_len, dtype=jnp.float32)
    growth = jnp.exp(rate_table[:, :, None] * offsets)
    shrink = jnp.exp(-rate_table[:, :, None] * offsets)
    lifted = signal.reshape(channels, 1, blocks, block_len) * growth[:, :, None, :]
    triangle = (offsets[None, :] <= offsets[:, None]).astype(jnp.float32)
    inside = (
        jnp.einsum("cnks,ts->cnkt", lifted, triangle, precision=highest) * shrink[:, :, None, :]
    )
    block_decay = jnp.exp(-rate_table * block_len)
    span_table = jnp.broadcast_to(block_decay[:, :, None], inside.shape[:3])
    factor, block_ends = lax.associative_scan(compose, (span_table, inside[..., -1]), axis=2)
    before = jnp.concatenate([jnp.zeros_like(block_ends[..., :1]), block_ends[..., :-1]], axis=2)
    carried_in = (
        jnp.exp(-rate_table[:, :, None] * (offsets + 1.0))[:, :, None, :] * before[..., None]
    )
    states = inside + carried_in
    return (states.reshape(channels, mode_count, length), block_ends[..., -1])


def short_forward(streams, tap_table, history):
    tap_count = tap_table.shape[-1]
    length = streams.shape[-1]
    extended = jnp.concatenate([history, streams], axis=-1)
    summed = jnp.zeros_like(streams)
    for tap_index in range(tap_count):
        begin_at = tap_count - 1 - tap_index
        summed = (
            summed
            + tap_table[..., tap_index : tap_index + 1]
            * extended[..., begin_at : begin_at + length]
        )
    return (summed, extended)


def short_backward(stream_grads, tap_table, future):
    tap_count = tap_table.shape[-1]
    length = stream_grads.shape[-1]
    extended = jnp.concatenate([stream_grads, future], axis=-1)
    summed = jnp.zeros_like(stream_grads)
    for tap_index in range(tap_count):
        summed = (
            summed
            + tap_table[..., tap_index : tap_index + 1]
            * extended[..., tap_index : tap_index + length]
        )
    return summed


def tap_grads(stream_grads, extended, tap_count):
    length = stream_grads.shape[-1]
    columns = []
    for tap_index in range(tap_count):
        begin_at = tap_count - 1 - tap_index
        columns.append(jnp.sum(stream_grads * extended[..., begin_at : begin_at + length], axis=-1))
    return jnp.stack(columns, axis=-1)


def core_backward(
    streams,
    cotangent,
    tap_table,
    residue_table,
    rate_table,
    skip_table,
    history,
    join_forward,
    join_reverse,
    fetch_future,
):
    tap_count = tap_table.shape[-1]
    features, extended = short_forward(streams, tap_table, history)
    query_feat, key_feat, value_feat = (features[0], features[1], features[2])
    mixed_input = key_feat * value_feat
    states, forward_end = modal_states(mixed_input, rate_table)
    states = states + join_forward(forward_end)
    conv_out = jnp.sum(residue_table[:, :, None] * states, axis=1)
    grad_query = cotangent * (conv_out + skip_table[:, None] * mixed_input)
    grad_conv = cotangent * query_feat
    reversed_states, reverse_end = modal_states(grad_conv[:, ::-1], rate_table)
    reversed_states = reversed_states + join_reverse(reverse_end)
    folded_back = jnp.sum(residue_table[:, :, None] * reversed_states, axis=1)[:, ::-1]
    grad_mixed = folded_back + skip_table[:, None] * grad_conv
    grad_residues = jnp.sum(mixed_input[:, None, ::-1] * reversed_states, axis=2)
    grad_skip = jnp.sum(grad_conv * mixed_input, axis=1)
    stream_grads = jnp.stack([grad_query, grad_mixed * value_feat, grad_mixed * key_feat])
    future = fetch_future(stream_grads[..., : tap_count - 1])
    pre_grads = short_backward(stream_grads, tap_table, future)
    grad_taps = tap_grads(stream_grads, extended, tap_count)
    return (pre_grads, grad_residues, grad_skip, grad_taps)


def on_device(
    query_pre, key_pre, value_pre, grad_out, w_value, short_taps, residues, decay_rates, skip
):
    tap_count = short_taps.shape[2]
    stacked_in = jnp.stack([query_pre.T, key_pre.T, value_pre.T, grad_out.T])
    gathered_in = lax.all_to_all(stacked_in, "ctx", split_axis=1, concat_axis=2, tiled=True)
    regrouped = (gathered_in[0], gathered_in[1], gathered_in[2], gathered_in[3])
    local_chans = regrouped[0].shape[0]
    begin_at = lax.axis_index("ctx") * local_chans

    def own_rows(table):
        return lax.dynamic_slice_in_dim(table, begin_at, local_chans, 0)

    taps_here = jnp.transpose(own_rows(short_taps), (1, 0, 2))
    streams = jnp.stack([regrouped[0], regrouped[1], regrouped[2]]).astype(jnp.float32)
    history = jnp.zeros(streams.shape[:2] + (tap_count - 1,), jnp.float32)

    def no_carry(end_state):
        return 0.0

    def no_future(head_rows):
        return jnp.zeros_like(head_rows)

    pre_grads, part_residues, part_skip, part_taps = core_backward(
        streams,
        regrouped[3].astype(jnp.float32),
        taps_here,
        own_rows(residues),
        own_rows(decay_rates),
        own_rows(skip),
        history,
        no_carry,
        no_carry,
        no_future,
    )
    rounded = pre_grads.astype(jnp.bfloat16)
    returned = lax.all_to_all(rounded, "ctx", split_axis=2, concat_axis=1, tiled=True)
    query_grad = returned[0].T
    key_grad = returned[1].T
    value_grad = returned[2].T
    owners = lax.axis_size("ctx")
    local_rows = part_residues.shape[0]
    packed = jnp.concatenate(
        [
            part_residues,
            part_skip[:, None],
            jnp.transpose(part_taps, (1, 0, 2)).reshape(local_rows, -1),
        ],
        axis=1,
    )
    spread = jnp.broadcast_to(packed[None], (owners,) + packed.shape)
    everyone = lax.all_to_all(spread, "ctx", split_axis=0, concat_axis=0, tiled=True)
    everyone = everyone.reshape(owners * local_rows, packed.shape[1])
    mode_count = part_residues.shape[1]
    d_residues = everyone[:, :mode_count]
    d_skip = everyone[:, mode_count]
    d_taps = everyone[:, mode_count + 1 :].reshape(-1, part_taps.shape[0], tap_count)
    partial_sum = lax.dot_general(
        value_grad, w_value, (((1,), (1,)), ((), ())), preferred_element_type=jnp.float32
    )
    narrowed = lax.optimization_barrier(partial_sum.astype(jnp.bfloat16))
    input_grad = lax.psum_scatter(
        narrowed.astype(jnp.float32).astype(jnp.bfloat16), "tp", scatter_dimension=0, tiled=True
    )
    return (input_grad, query_grad, key_grad, d_residues, d_skip, d_taps)


def solution(mesh):
    in_specs = (
        P("ctx", "tp"),
        P("ctx", "tp"),
        P("ctx", "tp"),
        P("ctx", "tp"),
        P(None, "tp"),
        P("tp", None, None),
        P("tp", None),
        P("tp", None),
        P("tp"),
    )
    out_specs = (
        P(("ctx", "tp"), None),
        P("ctx", "tp"),
        P("ctx", "tp"),
        P("tp", None),
        P("tp"),
        P("tp", None, None),
    )
    return jax.shard_map(
        on_device, mesh=mesh, in_specs=in_specs, out_specs=out_specs, check_vma=False
    )
```

```python
import jax
import jax.numpy as jnp
from jax import lax
from jax.sharding import PartitionSpec as P

highest = lax.Precision.HIGHEST


def compose(earlier, later):
    return (earlier[0] * later[0], later[0] * earlier[1] + later[1])


def modal_states(signal, rate_table):
    channels, length = signal.shape
    mode_count = rate_table.shape[1]
    block_len = min(128, length)
    blocks = length // block_len
    offsets = jnp.arange(block_len, dtype=jnp.float32)
    growth = jnp.exp(rate_table[:, :, None] * offsets)
    shrink = jnp.exp(-rate_table[:, :, None] * offsets)
    lifted = signal.reshape(channels, 1, blocks, block_len) * growth[:, :, None, :]
    triangle = (offsets[None, :] <= offsets[:, None]).astype(jnp.float32)
    inside = (
        jnp.einsum("cnks,ts->cnkt", lifted, triangle, precision=highest) * shrink[:, :, None, :]
    )
    block_decay = jnp.exp(-rate_table * block_len)
    span_table = jnp.broadcast_to(block_decay[:, :, None], inside.shape[:3])
    factor, block_ends = lax.associative_scan(compose, (span_table, inside[..., -1]), axis=2)
    before = jnp.concatenate([jnp.zeros_like(block_ends[..., :1]), block_ends[..., :-1]], axis=2)
    carried_in = (
        jnp.exp(-rate_table[:, :, None] * (offsets + 1.0))[:, :, None, :] * before[..., None]
    )
    states = inside + carried_in
    return (states.reshape(channels, mode_count, length), block_ends[..., -1])


def short_forward(streams, tap_table, history):
    tap_count = tap_table.shape[-1]
    length = streams.shape[-1]
    extended = jnp.concatenate([history, streams], axis=-1)
    summed = jnp.zeros_like(streams)
    for tap_index in range(tap_count):
        begin_at = tap_count - 1 - tap_index
        summed = (
            summed
            + tap_table[..., tap_index : tap_index + 1]
            * extended[..., begin_at : begin_at + length]
        )
    return (summed, extended)


def short_backward(stream_grads, tap_table, future):
    tap_count = tap_table.shape[-1]
    length = stream_grads.shape[-1]
    extended = jnp.concatenate([stream_grads, future], axis=-1)
    summed = jnp.zeros_like(stream_grads)
    for tap_index in range(tap_count):
        summed = (
            summed
            + tap_table[..., tap_index : tap_index + 1]
            * extended[..., tap_index : tap_index + length]
        )
    return summed


def tap_grads(stream_grads, extended, tap_count):
    length = stream_grads.shape[-1]
    columns = []
    for tap_index in range(tap_count):
        begin_at = tap_count - 1 - tap_index
        columns.append(jnp.sum(stream_grads * extended[..., begin_at : begin_at + length], axis=-1))
    return jnp.stack(columns, axis=-1)


def blocked_backward(pres, cotangent, taps, residue_table, rate_table, skip_table):
    tap_count = taps.shape[-1]
    chans, length = cotangent.shape
    block_len = min(128, length)
    blocks = length // block_len

    def delayed(values_in, amount):
        return jnp.pad(values_in, ((0, 0), (amount, 0)))[:, :length]

    def advance(values_in, amount):
        return jnp.pad(values_in, ((0, 0), (0, amount)))[:, amount:]

    feats = []
    for m in range(3):
        acc = taps[m][:, 0:1] * pres[m]
        for j in range(1, tap_count):
            acc = acc + taps[m][:, j : j + 1] * delayed(pres[m], j)
        feats.append(acc)
    query_feat, key_feat, value_feat = feats
    mixed = key_feat * value_feat
    grad_conv = cotangent * query_feat

    rate = rate_table[:, :, None]
    offs = jnp.arange(block_len, dtype=jnp.float32)
    up = jnp.exp(-rate * offs)
    down = jnp.exp(rate * offs)
    tri = (offs[:, None] <= offs[None, :]).astype(jnp.float32)
    toeplitz = (
        jnp.einsum("cns,cnt->cst", residue_table[:, :, None] * down, up, precision=highest) * tri
    )
    xb = mixed.reshape(chans, blocks, block_len)
    gb = grad_conv.reshape(chans, blocks, block_len)

    idx = jnp.arange(blocks, dtype=jnp.float32)
    gap = idx[:, None] - 1.0 - idx[None, :]
    carry_mat = jnp.where(
        gap >= 0, jnp.exp(-rate[..., None] * block_len * jnp.maximum(gap, 0.0)), 0.0
    )

    conv_intra = jnp.einsum("cks,cst->ckt", xb, toeplitz, precision=highest)
    tail_w = jnp.exp(-rate * (block_len - 1 - offs))
    ends = jnp.einsum("cks,cns->cnk", xb, tail_w, precision=highest)
    carried = jnp.einsum("cnkj,cnj->cnk", carry_mat, ends, precision=highest)
    lead_w = residue_table[:, :, None] * jnp.exp(-rate * (offs + 1.0))
    conv_carry = jnp.einsum("cnk,cnt->ckt", carried, lead_w, precision=highest)
    conv_out = (conv_intra + conv_carry).reshape(chans, length)

    back_intra = jnp.einsum("ckt,cst->cks", gb, toeplitz, precision=highest)
    starts = jnp.einsum("ckt,cnt->cnk", gb, up, precision=highest)
    later = jnp.einsum("cnjk,cnj->cnk", carry_mat, starts, precision=highest)
    back_w = jnp.exp(-rate * (block_len - offs))
    back_carry = jnp.einsum(
        "cnk,cns->cks", later, residue_table[:, :, None] * back_w, precision=highest
    )
    grad_mixed = (back_intra + back_carry).reshape(chans, length) + skip_table[:, None] * grad_conv

    pairs = jnp.einsum("cks,ckt->cst", xb, gb, precision=highest) * tri
    paired = jnp.einsum("cst,cnt->cns", pairs, up, precision=highest)
    res_intra = jnp.sum(paired * down, axis=2)
    lead_sums = jnp.einsum("cks,cns->cnk", xb, back_w, precision=highest)
    grad_residues = res_intra + jnp.sum(later * lead_sums, axis=2)
    grad_skip = jnp.sum(grad_conv * mixed, axis=1)

    grad_query = cotangent * (conv_out + skip_table[:, None] * mixed)
    stream_grads = (grad_query, grad_mixed * value_feat, grad_mixed * key_feat)
    pre_grads = []
    tap_cols = []
    for m in range(3):
        acc = taps[m][:, 0:1] * stream_grads[m]
        for j in range(1, tap_count):
            acc = acc + taps[m][:, j : j + 1] * advance(stream_grads[m], j)
        pre_grads.append(acc)
        tap_cols.append(
            jnp.stack(
                [jnp.sum(stream_grads[m] * delayed(pres[m], j), axis=1) for j in range(tap_count)],
                axis=-1,
            )
        )
    return (jnp.stack(pre_grads), grad_residues, grad_skip, jnp.stack(tap_cols))


def on_device(
    query_pre, key_pre, value_pre, grad_out, w_value, short_taps, residues, decay_rates, skip
):
    tap_count = short_taps.shape[2]
    stacked_in = jnp.stack([query_pre.T, key_pre.T, value_pre.T, grad_out.T])
    gathered_in = lax.all_to_all(stacked_in, "ctx", split_axis=1, concat_axis=2, tiled=True)
    regrouped = (gathered_in[0], gathered_in[1], gathered_in[2], gathered_in[3])
    local_chans = regrouped[0].shape[0]
    begin_at = lax.axis_index("ctx") * local_chans

    def own_rows(table):
        return lax.dynamic_slice_in_dim(table, begin_at, local_chans, 0)

    taps_here = jnp.transpose(own_rows(short_taps), (1, 0, 2))
    pre_grads, part_residues, part_skip, part_taps = blocked_backward(
        (
            regrouped[0].astype(jnp.float32),
            regrouped[1].astype(jnp.float32),
            regrouped[2].astype(jnp.float32),
        ),
        regrouped[3].astype(jnp.float32),
        taps_here,
        own_rows(residues),
        own_rows(decay_rates),
        own_rows(skip),
    )
    rounded = pre_grads.astype(jnp.bfloat16)
    returned = lax.all_to_all(rounded, "ctx", split_axis=2, concat_axis=1, tiled=True)
    query_grad = returned[0].T
    key_grad = returned[1].T
    value_grad = returned[2].T
    owners = lax.axis_size("ctx")
    local_rows = part_residues.shape[0]
    packed = jnp.concatenate(
        [
            part_residues,
            part_skip[:, None],
            jnp.transpose(part_taps, (1, 0, 2)).reshape(local_rows, -1),
        ],
        axis=1,
    )
    spread = jnp.broadcast_to(packed[None], (owners,) + packed.shape)
    everyone = lax.all_to_all(spread, "ctx", split_axis=0, concat_axis=0, tiled=True)
    everyone = everyone.reshape(owners * local_rows, packed.shape[1])
    mode_count = part_residues.shape[1]
    d_residues = everyone[:, :mode_count]
    d_skip = everyone[:, mode_count]
    d_taps = everyone[:, mode_count + 1 :].reshape(-1, part_taps.shape[0], tap_count)
    partial_sum = lax.dot_general(
        value_grad, w_value, (((1,), (1,)), ((), ())), preferred_element_type=jnp.float32
    )
    narrowed = lax.optimization_barrier(partial_sum.astype(jnp.bfloat16))
    input_grad = lax.psum_scatter(
        narrowed.astype(jnp.float32).astype(jnp.bfloat16), "tp", scatter_dimension=0, tiled=True
    )
    return (input_grad, query_grad, key_grad, d_residues, d_skip, d_taps)


def solution(mesh):
    in_specs = (
        P("ctx", "tp"),
        P("ctx", "tp"),
        P("ctx", "tp"),
        P("ctx", "tp"),
        P(None, "tp"),
        P("tp", None, None),
        P("tp", None),
        P("tp", None),
        P("tp"),
    )
    out_specs = (
        P(("ctx", "tp"), None),
        P("ctx", "tp"),
        P("ctx", "tp"),
        P("tp", None),
        P("tp"),
        P("tp", None, None),
    )
    return jax.shard_map(
        on_device, mesh=mesh, in_specs=in_specs, out_specs=out_specs, check_vma=False
    )
```

```python
import jax
import jax.numpy as jnp
from jax import lax
from jax.sharding import PartitionSpec as P

highest = lax.Precision.HIGHEST


def compose(earlier, later):
    return (earlier[0] * later[0], later[0] * earlier[1] + later[1])


def modal_states(signal, rate_table):
    channels, length = signal.shape
    mode_count = rate_table.shape[1]
    block_len = min(128, length)
    blocks = length // block_len
    offsets = jnp.arange(block_len, dtype=jnp.float32)
    growth = jnp.exp(rate_table[:, :, None] * offsets)
    shrink = jnp.exp(-rate_table[:, :, None] * offsets)
    lifted = signal.reshape(channels, 1, blocks, block_len) * growth[:, :, None, :]
    triangle = (offsets[None, :] <= offsets[:, None]).astype(jnp.float32)
    inside = (
        jnp.einsum("cnks,ts->cnkt", lifted, triangle, precision=highest) * shrink[:, :, None, :]
    )
    block_decay = jnp.exp(-rate_table * block_len)
    span_table = jnp.broadcast_to(block_decay[:, :, None], inside.shape[:3])
    factor, block_ends = lax.associative_scan(compose, (span_table, inside[..., -1]), axis=2)
    before = jnp.concatenate([jnp.zeros_like(block_ends[..., :1]), block_ends[..., :-1]], axis=2)
    carried_in = (
        jnp.exp(-rate_table[:, :, None] * (offsets + 1.0))[:, :, None, :] * before[..., None]
    )
    states = inside + carried_in
    return (states.reshape(channels, mode_count, length), block_ends[..., -1])


def short_forward(streams, tap_table, history):
    tap_count = tap_table.shape[-1]
    length = streams.shape[-1]
    extended = jnp.concatenate([history, streams], axis=-1)
    summed = jnp.zeros_like(streams)
    for tap_index in range(tap_count):
        begin_at = tap_count - 1 - tap_index
        summed = (
            summed
            + tap_table[..., tap_index : tap_index + 1]
            * extended[..., begin_at : begin_at + length]
        )
    return (summed, extended)


def short_backward(stream_grads, tap_table, future):
    tap_count = tap_table.shape[-1]
    length = stream_grads.shape[-1]
    extended = jnp.concatenate([stream_grads, future], axis=-1)
    summed = jnp.zeros_like(stream_grads)
    for tap_index in range(tap_count):
        summed = (
            summed
            + tap_table[..., tap_index : tap_index + 1]
            * extended[..., tap_index : tap_index + length]
        )
    return summed


def tap_grads(stream_grads, extended, tap_count):
    length = stream_grads.shape[-1]
    columns = []
    for tap_index in range(tap_count):
        begin_at = tap_count - 1 - tap_index
        columns.append(jnp.sum(stream_grads * extended[..., begin_at : begin_at + length], axis=-1))
    return jnp.stack(columns, axis=-1)


def blocked_backward(pres, cotangent, taps, residue_table, rate_table, skip_table):
    tap_count = taps.shape[-1]
    blocks, chans, block_len = cotangent.shape

    def delayed(values_in, amount):
        prev = jnp.pad(values_in[:-1], ((1, 0), (0, 0), (0, 0)))
        return jnp.concatenate(
            [prev[:, :, block_len - amount :], values_in[:, :, : block_len - amount]], axis=2
        )

    def advance(values_in, amount):
        nxt = jnp.pad(values_in[1:], ((0, 1), (0, 0), (0, 0)))
        return jnp.concatenate([values_in[:, :, amount:], nxt[:, :, :amount]], axis=2)

    def per_chan(column):
        return column[None, :, None]

    feats = []
    for m in range(3):
        acc = per_chan(taps[m][:, 0]) * pres[m]
        for j in range(1, tap_count):
            acc = acc + per_chan(taps[m][:, j]) * delayed(pres[m], j)
        feats.append(acc)
    query_feat, key_feat, value_feat = feats
    xb = key_feat * value_feat
    gb = cotangent * query_feat
    skip_b = per_chan(skip_table)

    rate = rate_table[:, :, None]
    offs = jnp.arange(block_len, dtype=jnp.float32)
    up = jnp.exp(-rate * offs)
    down = jnp.exp(rate * offs)
    tri = (offs[:, None] <= offs[None, :]).astype(jnp.float32)
    toeplitz = (
        jnp.einsum("cns,cnt->cst", residue_table[:, :, None] * down, up, precision=highest) * tri
    )

    idx = jnp.arange(blocks, dtype=jnp.float32)
    gap = idx[:, None] - 1.0 - idx[None, :]
    carry_mat = jnp.where(
        gap >= 0, jnp.exp(-rate[..., None] * block_len * jnp.maximum(gap, 0.0)), 0.0
    )

    conv_intra = jnp.einsum("kcs,cst->kct", xb, toeplitz, precision=highest)
    tail_w = jnp.exp(-rate * (block_len - 1 - offs))
    ends = jnp.einsum("kcs,cns->cnk", xb, tail_w, precision=highest)
    carried = jnp.sum(carry_mat * ends[:, :, None, :], axis=3)
    lead_w = residue_table[:, :, None] * jnp.exp(-rate * (offs + 1.0))
    conv_carry = jnp.einsum("cnk,cnt->kct", carried, lead_w, precision=highest)
    conv_out = conv_intra + conv_carry

    back_intra = jnp.einsum("kct,cst->kcs", gb, toeplitz, precision=highest)
    starts = jnp.einsum("kct,cnt->cnk", gb, up, precision=highest)
    later = jnp.sum(carry_mat * starts[:, :, :, None], axis=2)
    back_w = jnp.exp(-rate * (block_len - offs))
    back_carry = jnp.einsum(
        "cnk,cns->kcs", later, residue_table[:, :, None] * back_w, precision=highest
    )
    grad_mixed = back_intra + back_carry + skip_b * gb

    pairs = jnp.einsum("kcs,kct->cst", xb, gb, precision=highest) * tri
    paired = jnp.einsum("cst,cnt->cns", pairs, up, precision=highest)
    res_intra = jnp.sum(paired * down, axis=2)
    lead_sums = jnp.einsum("kcs,cns->cnk", xb, back_w, precision=highest)
    grad_residues = res_intra + jnp.sum(later * lead_sums, axis=2)
    grad_skip = jnp.sum(gb * xb, axis=(0, 2))

    grad_query = cotangent * (conv_out + skip_b * xb)
    stream_grads = (grad_query, grad_mixed * value_feat, grad_mixed * key_feat)
    pre_grads = []
    tap_cols = []
    for m in range(3):
        acc = per_chan(taps[m][:, 0]) * stream_grads[m]
        for j in range(1, tap_count):
            acc = acc + per_chan(taps[m][:, j]) * advance(stream_grads[m], j)
        pre_grads.append(acc)
        tap_cols.append(
            jnp.stack(
                [jnp.sum(stream_grads[m] * pres[m], axis=(0, 2))]
                + [
                    jnp.sum(stream_grads[m] * delayed(pres[m], j), axis=(0, 2))
                    for j in range(1, tap_count)
                ],
                axis=-1,
            )
        )
    return (jnp.stack(pre_grads, axis=1), grad_residues, grad_skip, jnp.stack(tap_cols))


def on_device(
    query_pre, key_pre, value_pre, grad_out, w_value, short_taps, residues, decay_rates, skip
):
    tap_count = short_taps.shape[2]
    owners = lax.axis_size("ctx")
    tokens_here, chans_here = query_pre.shape
    local_chans = chans_here // owners

    def to_owner_form(values_in):
        return jnp.transpose(values_in.reshape(tokens_here, owners, local_chans), (1, 2, 0))

    stacked_in = jnp.stack(
        [to_owner_form(query_pre), to_owner_form(key_pre), to_owner_form(value_pre), to_owner_form(grad_out)],
        axis=1,
    )
    gathered_in = lax.all_to_all(stacked_in, "ctx", split_axis=0, concat_axis=0, tiled=True)
    regrouped = tuple(gathered_in[:, i].astype(jnp.float32) for i in range(4))
    begin_at = lax.axis_index("ctx") * local_chans

    def own_rows(table):
        return lax.dynamic_slice_in_dim(table, begin_at, local_chans, 0)

    taps_here = jnp.transpose(own_rows(short_taps), (1, 0, 2))
    pre_grads, part_residues, part_skip, part_taps = blocked_backward(
        (regrouped[0], regrouped[1], regrouped[2]),
        regrouped[3],
        taps_here,
        own_rows(residues),
        own_rows(decay_rates),
        own_rows(skip),
    )
    rounded = pre_grads.astype(jnp.bfloat16)
    returned = lax.all_to_all(rounded, "ctx", split_axis=0, concat_axis=0, tiled=True)
    flat = jnp.transpose(returned, (1, 3, 0, 2)).reshape(3, tokens_here, chans_here)
    query_grad = flat[0]
    key_grad = flat[1]
    value_grad = flat[2]
    local_rows = part_residues.shape[0]
    packed = jnp.concatenate(
        [
            part_residues,
            part_skip[:, None],
            jnp.transpose(part_taps, (1, 0, 2)).reshape(local_rows, -1),
        ],
        axis=1,
    )
    spread = jnp.broadcast_to(packed[None], (owners,) + packed.shape)
    everyone = lax.all_to_all(spread, "ctx", split_axis=0, concat_axis=0, tiled=True)
    everyone = everyone.reshape(owners * local_rows, packed.shape[1])
    mode_count = part_residues.shape[1]
    d_residues = everyone[:, :mode_count]
    d_skip = everyone[:, mode_count]
    d_taps = everyone[:, mode_count + 1 :].reshape(-1, part_taps.shape[0], tap_count)
    partial_sum = lax.dot_general(
        value_grad, w_value, (((1,), (1,)), ((), ())), preferred_element_type=jnp.float32
    )
    narrowed = lax.optimization_barrier(partial_sum.astype(jnp.bfloat16))
    input_grad = lax.psum_scatter(
        narrowed.astype(jnp.float32).astype(jnp.bfloat16), "tp", scatter_dimension=0, tiled=True
    )
    return (input_grad, query_grad, key_grad, d_residues, d_skip, d_taps)


def solution(mesh):
    in_specs = (
        P("ctx", "tp"),
        P("ctx", "tp"),
        P("ctx", "tp"),
        P("ctx", "tp"),
        P(None, "tp"),
        P("tp", None, None),
        P("tp", None),
        P("tp", None),
        P("tp"),
    )
    out_specs = (
        P(("ctx", "tp"), None),
        P("ctx", "tp"),
        P("ctx", "tp"),
        P("tp", None),
        P("tp"),
        P("tp", None, None),
    )
    return jax.shard_map(
        on_device, mesh=mesh, in_specs=in_specs, out_specs=out_specs, check_vma=False
    )
```

```python
import jax
import jax.numpy as jnp
from jax import lax
from jax.sharding import PartitionSpec as P

highest = lax.Precision.HIGHEST


def compose(earlier, later):
    return (earlier[0] * later[0], later[0] * earlier[1] + later[1])


def modal_states(signal, rate_table):
    channels, length = signal.shape
    mode_count = rate_table.shape[1]
    block_len = min(128, length)
    blocks = length // block_len
    offsets = jnp.arange(block_len, dtype=jnp.float32)
    growth = jnp.exp(rate_table[:, :, None] * offsets)
    shrink = jnp.exp(-rate_table[:, :, None] * offsets)
    lifted = signal.reshape(channels, 1, blocks, block_len) * growth[:, :, None, :]
    triangle = (offsets[None, :] <= offsets[:, None]).astype(jnp.float32)
    inside = (
        jnp.einsum("cnks,ts->cnkt", lifted, triangle, precision=highest) * shrink[:, :, None, :]
    )
    block_decay = jnp.exp(-rate_table * block_len)
    span_table = jnp.broadcast_to(block_decay[:, :, None], inside.shape[:3])
    factor, block_ends = lax.associative_scan(compose, (span_table, inside[..., -1]), axis=2)
    before = jnp.concatenate([jnp.zeros_like(block_ends[..., :1]), block_ends[..., :-1]], axis=2)
    carried_in = (
        jnp.exp(-rate_table[:, :, None] * (offsets + 1.0))[:, :, None, :] * before[..., None]
    )
    states = inside + carried_in
    return (states.reshape(channels, mode_count, length), block_ends[..., -1])


def short_forward(streams, tap_table, history):
    tap_count = tap_table.shape[-1]
    length = streams.shape[-1]
    extended = jnp.concatenate([history, streams], axis=-1)
    summed = jnp.zeros_like(streams)
    for tap_index in range(tap_count):
        begin_at = tap_count - 1 - tap_index
        summed = (
            summed
            + tap_table[..., tap_index : tap_index + 1]
            * extended[..., begin_at : begin_at + length]
        )
    return (summed, extended)


def short_backward(stream_grads, tap_table, future):
    tap_count = tap_table.shape[-1]
    length = stream_grads.shape[-1]
    extended = jnp.concatenate([stream_grads, future], axis=-1)
    summed = jnp.zeros_like(stream_grads)
    for tap_index in range(tap_count):
        summed = (
            summed
            + tap_table[..., tap_index : tap_index + 1]
            * extended[..., tap_index : tap_index + length]
        )
    return summed


def tap_grads(stream_grads, extended, tap_count):
    length = stream_grads.shape[-1]
    columns = []
    for tap_index in range(tap_count):
        begin_at = tap_count - 1 - tap_index
        columns.append(jnp.sum(stream_grads * extended[..., begin_at : begin_at + length], axis=-1))
    return jnp.stack(columns, axis=-1)


def blocked_backward(pres, cotangent, taps, residue_table, rate_table, skip_table):
    tap_count = taps.shape[-1]
    blocks, chans, block_len = cotangent.shape

    def delayed(values_in, amount):
        prev = jnp.pad(values_in[:-1], ((1, 0), (0, 0), (0, 0)))
        return jnp.concatenate(
            [prev[:, :, block_len - amount :], values_in[:, :, : block_len - amount]], axis=2
        )

    def advance(values_in, amount):
        nxt = jnp.pad(values_in[1:], ((0, 1), (0, 0), (0, 0)))
        return jnp.concatenate([values_in[:, :, amount:], nxt[:, :, :amount]], axis=2)

    def per_chan(column):
        return column[None, :, None]

    feats = []
    for m in range(3):
        acc = per_chan(taps[m][:, 0]) * pres[m]
        for j in range(1, tap_count):
            acc = acc + per_chan(taps[m][:, j]) * delayed(pres[m], j)
        feats.append(acc)
    query_feat, key_feat, value_feat = feats
    xb = key_feat * value_feat
    gb = cotangent * query_feat
    skip_b = per_chan(skip_table)

    rate = rate_table[:, :, None]
    offs = jnp.arange(block_len, dtype=jnp.float32)
    up = jnp.exp(-rate * offs)
    down = jnp.exp(rate * offs)
    tri = (offs[:, None] <= offs[None, :]).astype(jnp.float32)
    toeplitz = (
        jnp.einsum("cns,cnt->cst", residue_table[:, :, None] * down, up, precision=highest) * tri
    )

    idx = jnp.arange(blocks, dtype=jnp.float32)
    gap = idx[:, None] - 1.0 - idx[None, :]
    carry_mat = jnp.where(
        gap >= 0, jnp.exp(-rate[..., None] * block_len * jnp.maximum(gap, 0.0)), 0.0
    )

    conv_intra = jnp.einsum("kcs,cst->kct", xb, toeplitz, precision=highest)
    tail_w = jnp.exp(-rate * (block_len - 1 - offs))
    ends = jnp.einsum("kcs,cns->cnk", xb, tail_w, precision=highest)
    carried = jnp.sum(carry_mat * ends[:, :, None, :], axis=3)
    lead_w = residue_table[:, :, None] * jnp.exp(-rate * (offs + 1.0))
    conv_carry = jnp.einsum("cnk,cnt->kct", carried, lead_w, precision=highest)
    conv_out = conv_intra + conv_carry

    back_intra = jnp.einsum("kct,cst->kcs", gb, toeplitz, precision=highest)
    starts = jnp.einsum("kct,cnt->cnk", gb, up, precision=highest)
    later = jnp.sum(carry_mat * starts[:, :, :, None], axis=2)
    back_w = jnp.exp(-rate * (block_len - offs))
    back_carry = jnp.einsum(
        "cnk,cns->kcs", later, residue_table[:, :, None] * back_w, precision=highest
    )
    grad_mixed = back_intra + back_carry + skip_b * gb

    pairs = jnp.einsum("kcs,kct->cst", xb, gb, precision=highest) * tri
    paired = jnp.einsum("cst,cnt->cns", pairs, up, precision=highest)
    res_intra = jnp.sum(paired * down, axis=2)
    lead_sums = jnp.einsum("kcs,cns->cnk", xb, back_w, precision=highest)
    grad_residues = res_intra + jnp.sum(later * lead_sums, axis=2)
    grad_skip = jnp.sum(gb * xb, axis=(0, 2))

    grad_query = cotangent * (conv_out + skip_b * xb)
    stream_grads = (grad_query, grad_mixed * value_feat, grad_mixed * key_feat)
    pre_grads = []
    tap_cols = []
    for m in range(3):
        acc = per_chan(taps[m][:, 0]) * stream_grads[m]
        for j in range(1, tap_count):
            acc = acc + per_chan(taps[m][:, j]) * advance(stream_grads[m], j)
        pre_grads.append(acc)
        tap_cols.append(
            jnp.stack(
                [jnp.sum(stream_grads[m] * pres[m], axis=(0, 2))]
                + [
                    jnp.sum(stream_grads[m] * delayed(pres[m], j), axis=(0, 2))
                    for j in range(1, tap_count)
                ],
                axis=-1,
            )
        )
    return (jnp.stack(pre_grads, axis=1), grad_residues, grad_skip, jnp.stack(tap_cols))


def on_device(
    query_pre, key_pre, value_pre, grad_out, w_value, short_taps, residues, decay_rates, skip
):
    tap_count = short_taps.shape[2]
    owners = lax.axis_size("ctx")
    tokens_here, chans_here = query_pre.shape
    local_chans = chans_here // owners

    def to_owner_form(values_in):
        return jnp.transpose(values_in.reshape(tokens_here, owners, local_chans), (1, 2, 0))

    stacked_in = jnp.stack(
        [to_owner_form(query_pre), to_owner_form(key_pre), to_owner_form(value_pre), to_owner_form(grad_out)],
        axis=1,
    )
    gathered_in = lax.all_to_all(stacked_in, "ctx", split_axis=0, concat_axis=0, tiled=True)
    regrouped = tuple(gathered_in[:, i].astype(jnp.float32) for i in range(4))
    begin_at = lax.axis_index("ctx") * local_chans

    def own_rows(table):
        return lax.dynamic_slice_in_dim(table, begin_at, local_chans, 0)

    taps_here = jnp.transpose(own_rows(short_taps), (1, 0, 2))
    pre_grads, part_residues, part_skip, part_taps = blocked_backward(
        (regrouped[0], regrouped[1], regrouped[2]),
        regrouped[3],
        taps_here,
        own_rows(residues),
        own_rows(decay_rates),
        own_rows(skip),
    )
    local_rows = part_residues.shape[0]
    mode_count = part_residues.shape[1]
    packed = jnp.concatenate(
        [
            part_residues,
            part_skip[:, None],
            jnp.transpose(part_taps, (1, 0, 2)).reshape(local_rows, -1),
        ],
        axis=1,
    )
    packed_hi = packed.astype(jnp.bfloat16)
    packed_lo = (packed - packed_hi.astype(jnp.float32)).astype(jnp.bfloat16)
    split_pair = jnp.concatenate([packed_hi, packed_lo], axis=1).reshape(-1)
    lane_len = pre_grads.shape[-1]
    side_rows = -(-split_pair.shape[0] // lane_len)
    side_rows = -(-side_rows // 8) * 8
    side = jnp.pad(split_pair, (0, side_rows * lane_len - split_pair.shape[0])).reshape(side_rows, lane_len)
    rounded = pre_grads.astype(jnp.bfloat16)
    grad_rows = rounded.shape[1] * rounded.shape[2]
    payload = jnp.concatenate(
        [
            rounded.reshape(owners, grad_rows, lane_len),
            jnp.broadcast_to(side[None], (owners, side_rows, lane_len)),
        ],
        axis=1,
    )
    returned = lax.all_to_all(payload, "ctx", split_axis=0, concat_axis=0, tiled=True)
    grads_back = returned[:, :grad_rows].reshape(rounded.shape)
    flat = jnp.transpose(grads_back, (1, 3, 0, 2)).reshape(3, tokens_here, chans_here)
    query_grad = flat[0]
    key_grad = flat[1]
    value_grad = flat[2]
    width = packed.shape[1]
    side_back = returned[:, grad_rows:].reshape(owners, -1)[:, : split_pair.shape[0]]
    side_back = side_back.reshape(owners * local_rows, 2 * width).astype(jnp.float32)
    everyone = side_back[:, :width] + side_back[:, width:]
    d_residues = everyone[:, :mode_count]
    d_skip = everyone[:, mode_count]
    d_taps = everyone[:, mode_count + 1 :].reshape(-1, part_taps.shape[0], tap_count)
    partial_sum = lax.dot_general(
        value_grad, w_value, (((1,), (1,)), ((), ())), preferred_element_type=jnp.float32
    )
    narrowed = lax.optimization_barrier(partial_sum.astype(jnp.bfloat16))
    input_grad = lax.psum_scatter(
        narrowed.astype(jnp.float32).astype(jnp.bfloat16), "tp", scatter_dimension=0, tiled=True
    )
    return (input_grad, query_grad, key_grad, d_residues, d_skip, d_taps)


def solution(mesh):
    in_specs = (
        P("ctx", "tp"),
        P("ctx", "tp"),
        P("ctx", "tp"),
        P("ctx", "tp"),
        P(None, "tp"),
        P("tp", None, None),
        P("tp", None),
        P("tp", None),
        P("tp"),
    )
    out_specs = (
        P(("ctx", "tp"), None),
        P("ctx", "tp"),
        P("ctx", "tp"),
        P("tp", None),
        P("tp"),
        P("tp", None, None),
    )
    return jax.shard_map(
        on_device, mesh=mesh, in_specs=in_specs, out_specs=out_specs, check_vma=False
    )
```

```python
import jax
import jax.numpy as jnp
from jax import lax
from jax.sharding import PartitionSpec as P

highest = lax.Precision.HIGHEST


def compose(earlier, later):
    return (earlier[0] * later[0], later[0] * earlier[1] + later[1])


def modal_states(signal, rate_table):
    channels, length = signal.shape
    mode_count = rate_table.shape[1]
    block_len = min(128, length)
    blocks = length // block_len
    offsets = jnp.arange(block_len, dtype=jnp.float32)
    growth = jnp.exp(rate_table[:, :, None] * offsets)
    shrink = jnp.exp(-rate_table[:, :, None] * offsets)
    lifted = signal.reshape(channels, 1, blocks, block_len) * growth[:, :, None, :]
    triangle = (offsets[None, :] <= offsets[:, None]).astype(jnp.float32)
    inside = (
        jnp.einsum("cnks,ts->cnkt", lifted, triangle, precision=highest) * shrink[:, :, None, :]
    )
    block_decay = jnp.exp(-rate_table * block_len)
    span_table = jnp.broadcast_to(block_decay[:, :, None], inside.shape[:3])
    factor, block_ends = lax.associative_scan(compose, (span_table, inside[..., -1]), axis=2)
    before = jnp.concatenate([jnp.zeros_like(block_ends[..., :1]), block_ends[..., :-1]], axis=2)
    carried_in = (
        jnp.exp(-rate_table[:, :, None] * (offsets + 1.0))[:, :, None, :] * before[..., None]
    )
    states = inside + carried_in
    return (states.reshape(channels, mode_count, length), block_ends[..., -1])


def short_forward(streams, tap_table, history):
    tap_count = tap_table.shape[-1]
    length = streams.shape[-1]
    extended = jnp.concatenate([history, streams], axis=-1)
    summed = jnp.zeros_like(streams)
    for tap_index in range(tap_count):
        begin_at = tap_count - 1 - tap_index
        summed = (
            summed
            + tap_table[..., tap_index : tap_index + 1]
            * extended[..., begin_at : begin_at + length]
        )
    return (summed, extended)


def short_backward(stream_grads, tap_table, future):
    tap_count = tap_table.shape[-1]
    length = stream_grads.shape[-1]
    extended = jnp.concatenate([stream_grads, future], axis=-1)
    summed = jnp.zeros_like(stream_grads)
    for tap_index in range(tap_count):
        summed = (
            summed
            + tap_table[..., tap_index : tap_index + 1]
            * extended[..., tap_index : tap_index + length]
        )
    return summed


def tap_grads(stream_grads, extended, tap_count):
    length = stream_grads.shape[-1]
    columns = []
    for tap_index in range(tap_count):
        begin_at = tap_count - 1 - tap_index
        columns.append(jnp.sum(stream_grads * extended[..., begin_at : begin_at + length], axis=-1))
    return jnp.stack(columns, axis=-1)


def blocked_backward(pres, cotangent, taps, residue_table, rate_table, skip_table):
    tap_count = taps.shape[-1]
    blocks, chans, block_len = cotangent.shape

    def delayed(values_in, amount):
        prev = jnp.pad(values_in[:-1], ((1, 0), (0, 0), (0, 0)))
        return jnp.concatenate(
            [prev[:, :, block_len - amount :], values_in[:, :, : block_len - amount]], axis=2
        )

    def advance(values_in, amount):
        nxt = jnp.pad(values_in[1:], ((0, 1), (0, 0), (0, 0)))
        return jnp.concatenate([values_in[:, :, amount:], nxt[:, :, :amount]], axis=2)

    def per_chan(column):
        return column[None, :, None]

    feats = []
    for m in range(3):
        acc = per_chan(taps[m][:, 0]) * pres[m]
        for j in range(1, tap_count):
            acc = acc + per_chan(taps[m][:, j]) * delayed(pres[m], j)
        feats.append(acc)
    query_feat, key_feat, value_feat = feats
    xb = key_feat * value_feat
    gb = cotangent * query_feat
    skip_b = per_chan(skip_table)

    rate = rate_table[:, :, None]
    offs = jnp.arange(block_len, dtype=jnp.float32)
    up = jnp.exp(-rate * offs)
    down = jnp.exp(rate * offs)
    tri = (offs[:, None] <= offs[None, :]).astype(jnp.float32)
    toeplitz = (
        jnp.einsum("cns,cnt->cst", residue_table[:, :, None] * down, up, precision=highest) * tri
    )

    idx = jnp.arange(blocks, dtype=jnp.float32)
    gap = idx[:, None] - 1.0 - idx[None, :]
    carry_mat = jnp.where(
        gap >= 0, jnp.exp(-rate[..., None] * block_len * jnp.maximum(gap, 0.0)), 0.0
    )

    conv_intra = jnp.einsum("kcs,cst->kct", xb, toeplitz, precision=highest)
    tail_w = jnp.exp(-rate * (block_len - 1 - offs))
    ends = jnp.einsum("kcs,cns->cnk", xb, tail_w, precision=highest)
    carried = jnp.sum(carry_mat * ends[:, :, None, :], axis=3)
    lead_w = residue_table[:, :, None] * jnp.exp(-rate * (offs + 1.0))
    conv_carry = jnp.einsum("cnk,cnt->kct", carried, lead_w, precision=highest)
    conv_out = conv_intra + conv_carry

    back_intra = jnp.einsum("kct,cst->kcs", gb, toeplitz, precision=highest)
    starts = jnp.einsum("kct,cnt->cnk", gb, up, precision=highest)
    later = jnp.sum(carry_mat * starts[:, :, :, None], axis=2)
    back_w = jnp.exp(-rate * (block_len - offs))
    back_carry = jnp.einsum(
        "cnk,cns->kcs", later, residue_table[:, :, None] * back_w, precision=highest
    )
    grad_mixed = back_intra + back_carry + skip_b * gb

    pairs = jnp.einsum("kcs,kct->cst", xb, gb, precision=highest) * tri
    paired = jnp.einsum("cst,cnt->cns", pairs, up, precision=highest)
    res_intra = jnp.sum(paired * down, axis=2)
    lead_sums = jnp.einsum("kcs,cns->cnk", xb, back_w, precision=highest)
    grad_residues = res_intra + jnp.sum(later * lead_sums, axis=2)
    grad_skip = jnp.sum(gb * xb, axis=(0, 2))

    grad_query = cotangent * (conv_out + skip_b * xb)
    stream_grads = (grad_query, grad_mixed * value_feat, grad_mixed * key_feat)
    pre_grads = []
    tap_cols = []
    for m in range(3):
        acc = per_chan(taps[m][:, 0]) * stream_grads[m]
        for j in range(1, tap_count):
            acc = acc + per_chan(taps[m][:, j]) * advance(stream_grads[m], j)
        pre_grads.append(acc)
        tap_cols.append(
            jnp.stack(
                [jnp.sum(stream_grads[m] * pres[m], axis=(0, 2))]
                + [
                    jnp.sum(stream_grads[m] * delayed(pres[m], j), axis=(0, 2))
                    for j in range(1, tap_count)
                ],
                axis=-1,
            )
        )
    return (jnp.stack(pre_grads, axis=1), grad_residues, grad_skip, jnp.stack(tap_cols))


def ctx_exchange(values_in):
    hi = lax.axis_size("ctx_hi")
    lo = lax.axis_size("ctx_lo")
    rest = values_in.shape[1:]
    staged = values_in.reshape((hi, lo) + rest)
    staged = lax.all_to_all(staged, "ctx_lo", split_axis=1, concat_axis=1, tiled=True)
    staged = lax.all_to_all(staged, "ctx_hi", split_axis=0, concat_axis=0, tiled=True)
    return staged.reshape((hi * lo,) + rest)


def on_device(
    query_pre, key_pre, value_pre, grad_out, w_value, short_taps, residues, decay_rates, skip
):
    tap_count = short_taps.shape[2]
    owners = lax.axis_size("ctx_hi") * lax.axis_size("ctx_lo")
    tokens_here, chans_here = query_pre.shape
    local_chans = chans_here // owners

    def to_owner_form(values_in):
        return jnp.transpose(values_in.reshape(tokens_here, owners, local_chans), (1, 2, 0))

    stacked_in = jnp.stack(
        [to_owner_form(query_pre), to_owner_form(key_pre), to_owner_form(value_pre), to_owner_form(grad_out)],
        axis=1,
    )
    gathered_in = ctx_exchange(stacked_in)
    regrouped = tuple(gathered_in[:, i].astype(jnp.float32) for i in range(4))
    begin_at = (
        lax.axis_index("ctx_hi") * lax.axis_size("ctx_lo") + lax.axis_index("ctx_lo")
    ) * local_chans

    def own_rows(table):
        return lax.dynamic_slice_in_dim(table, begin_at, local_chans, 0)

    taps_here = jnp.transpose(own_rows(short_taps), (1, 0, 2))
    pre_grads, part_residues, part_skip, part_taps = blocked_backward(
        (regrouped[0], regrouped[1], regrouped[2]),
        regrouped[3],
        taps_here,
        own_rows(residues),
        own_rows(decay_rates),
        own_rows(skip),
    )
    rounded = pre_grads.astype(jnp.bfloat16)
    returned = ctx_exchange(rounded)
    flat = jnp.transpose(returned, (1, 3, 0, 2)).reshape(3, tokens_here, chans_here)
    query_grad = flat[0]
    key_grad = flat[1]
    value_grad = flat[2]
    local_rows = part_residues.shape[0]
    packed = jnp.concatenate(
        [
            part_residues,
            part_skip[:, None],
            jnp.transpose(part_taps, (1, 0, 2)).reshape(local_rows, -1),
        ],
        axis=1,
    )
    spread = jnp.broadcast_to(packed[None], (owners,) + packed.shape)
    everyone = ctx_exchange(spread)
    everyone = everyone.reshape(owners * local_rows, packed.shape[1])
    mode_count = part_residues.shape[1]
    d_residues = everyone[:, :mode_count]
    d_skip = everyone[:, mode_count]
    d_taps = everyone[:, mode_count + 1 :].reshape(-1, part_taps.shape[0], tap_count)
    partial_sum = lax.dot_general(
        value_grad, w_value, (((1,), (1,)), ((), ())), preferred_element_type=jnp.float32
    )
    narrowed = lax.optimization_barrier(partial_sum.astype(jnp.bfloat16))
    input_grad = lax.psum_scatter(
        narrowed.astype(jnp.float32).astype(jnp.bfloat16), "tp", scatter_dimension=0, tiled=True
    )
    return (input_grad, query_grad, key_grad, d_residues, d_skip, d_taps)


def solution(mesh):
    ctx_size = mesh.shape["ctx"]
    lo_size = 8 if ctx_size % 8 == 0 else 1
    split_mesh = jax.sharding.Mesh(
        mesh.devices.reshape(ctx_size // lo_size, lo_size, mesh.shape["tp"]),
        ("ctx_hi", "ctx_lo", "tp"),
    )
    ctx = ("ctx_hi", "ctx_lo")
    in_specs = (
        P(ctx, "tp"),
        P(ctx, "tp"),
        P(ctx, "tp"),
        P(ctx, "tp"),
        P(None, "tp"),
        P("tp", None, None),
        P("tp", None),
        P("tp", None),
        P("tp"),
    )
    out_specs = (
        P(("ctx_hi", "ctx_lo", "tp"), None),
        P(ctx, "tp"),
        P(ctx, "tp"),
        P("tp", None),
        P("tp"),
        P("tp", None, None),
    )
    return jax.shard_map(
        on_device, mesh=split_mesh, in_specs=in_specs, out_specs=out_specs, check_vma=False
    )
```

```python
import jax
import jax.numpy as jnp
from jax import lax
from jax.sharding import PartitionSpec as P

highest = lax.Precision.HIGHEST


def compose(earlier, later):
    return (earlier[0] * later[0], later[0] * earlier[1] + later[1])


def modal_states(signal, rate_table):
    channels, length = signal.shape
    mode_count = rate_table.shape[1]
    block_len = min(128, length)
    blocks = length // block_len
    offsets = jnp.arange(block_len, dtype=jnp.float32)
    growth = jnp.exp(rate_table[:, :, None] * offsets)
    shrink = jnp.exp(-rate_table[:, :, None] * offsets)
    lifted = signal.reshape(channels, 1, blocks, block_len) * growth[:, :, None, :]
    triangle = (offsets[None, :] <= offsets[:, None]).astype(jnp.float32)
    inside = (
        jnp.einsum("cnks,ts->cnkt", lifted, triangle, precision=highest) * shrink[:, :, None, :]
    )
    block_decay = jnp.exp(-rate_table * block_len)
    span_table = jnp.broadcast_to(block_decay[:, :, None], inside.shape[:3])
    factor, block_ends = lax.associative_scan(compose, (span_table, inside[..., -1]), axis=2)
    before = jnp.concatenate([jnp.zeros_like(block_ends[..., :1]), block_ends[..., :-1]], axis=2)
    carried_in = (
        jnp.exp(-rate_table[:, :, None] * (offsets + 1.0))[:, :, None, :] * before[..., None]
    )
    states = inside + carried_in
    return (states.reshape(channels, mode_count, length), block_ends[..., -1])


def short_forward(streams, tap_table, history):
    tap_count = tap_table.shape[-1]
    length = streams.shape[-1]
    extended = jnp.concatenate([history, streams], axis=-1)
    summed = jnp.zeros_like(streams)
    for tap_index in range(tap_count):
        begin_at = tap_count - 1 - tap_index
        summed = (
            summed
            + tap_table[..., tap_index : tap_index + 1]
            * extended[..., begin_at : begin_at + length]
        )
    return (summed, extended)


def short_backward(stream_grads, tap_table, future):
    tap_count = tap_table.shape[-1]
    length = stream_grads.shape[-1]
    extended = jnp.concatenate([stream_grads, future], axis=-1)
    summed = jnp.zeros_like(stream_grads)
    for tap_index in range(tap_count):
        summed = (
            summed
            + tap_table[..., tap_index : tap_index + 1]
            * extended[..., tap_index : tap_index + length]
        )
    return summed


def tap_grads(stream_grads, extended, tap_count):
    length = stream_grads.shape[-1]
    columns = []
    for tap_index in range(tap_count):
        begin_at = tap_count - 1 - tap_index
        columns.append(jnp.sum(stream_grads * extended[..., begin_at : begin_at + length], axis=-1))
    return jnp.stack(columns, axis=-1)


def blocked_backward(pres, cotangent, taps, residue_table, rate_table, skip_table):
    tap_count = taps.shape[-1]
    blocks, chans, block_len = cotangent.shape

    def delayed(values_in, amount):
        prev = jnp.pad(values_in[:-1], ((1, 0), (0, 0), (0, 0)))
        return jnp.concatenate(
            [prev[:, :, block_len - amount :], values_in[:, :, : block_len - amount]], axis=2
        )

    def advance(values_in, amount):
        nxt = jnp.pad(values_in[1:], ((0, 1), (0, 0), (0, 0)))
        return jnp.concatenate([values_in[:, :, amount:], nxt[:, :, :amount]], axis=2)

    def per_chan(column):
        return column[None, :, None]

    feats = []
    for m in range(3):
        acc = per_chan(taps[m][:, 0]) * pres[m]
        for j in range(1, tap_count):
            acc = acc + per_chan(taps[m][:, j]) * delayed(pres[m], j)
        feats.append(acc)
    query_feat, key_feat, value_feat = feats
    xb = key_feat * value_feat
    gb = cotangent * query_feat
    skip_b = per_chan(skip_table)

    rate = rate_table[:, :, None]
    offs = jnp.arange(block_len, dtype=jnp.float32)
    up = jnp.exp(-rate * offs)
    down = jnp.exp(rate * offs)
    tri = (offs[:, None] <= offs[None, :]).astype(jnp.float32)
    toeplitz = (
        jnp.einsum("cns,cnt->cst", residue_table[:, :, None] * down, up, precision=highest) * tri
    )

    idx = jnp.arange(blocks, dtype=jnp.float32)
    gap = idx[:, None] - 1.0 - idx[None, :]
    carry_mat = jnp.where(
        gap >= 0, jnp.exp(-rate[..., None] * block_len * jnp.maximum(gap, 0.0)), 0.0
    )

    conv_intra = jnp.einsum("kcs,cst->kct", xb, toeplitz, precision=highest)
    tail_w = jnp.exp(-rate * (block_len - 1 - offs))
    ends = jnp.einsum("kcs,cns->cnk", xb, tail_w, precision=highest)
    carried = jnp.sum(carry_mat * ends[:, :, None, :], axis=3)
    lead_w = residue_table[:, :, None] * jnp.exp(-rate * (offs + 1.0))
    conv_carry = jnp.einsum("cnk,cnt->kct", carried, lead_w, precision=highest)
    conv_out = conv_intra + conv_carry

    back_intra = jnp.einsum("kct,cst->kcs", gb, toeplitz, precision=highest)
    starts = jnp.einsum("kct,cnt->cnk", gb, up, precision=highest)
    later = jnp.sum(carry_mat * starts[:, :, :, None], axis=2)
    back_w = jnp.exp(-rate * (block_len - offs))
    back_carry = jnp.einsum(
        "cnk,cns->kcs", later, residue_table[:, :, None] * back_w, precision=highest
    )
    grad_mixed = back_intra + back_carry + skip_b * gb

    pairs = jnp.einsum("kcs,kct->cst", xb, gb, precision=highest) * tri
    paired = jnp.einsum("cst,cnt->cns", pairs, up, precision=highest)
    res_intra = jnp.sum(paired * down, axis=2)
    lead_sums = jnp.einsum("kcs,cns->cnk", xb, back_w, precision=highest)
    grad_residues = res_intra + jnp.sum(later * lead_sums, axis=2)
    grad_skip = jnp.sum(gb * xb, axis=(0, 2))

    grad_query = cotangent * (conv_out + skip_b * xb)
    stream_grads = (grad_query, grad_mixed * value_feat, grad_mixed * key_feat)
    pre_grads = []
    tap_cols = []
    for m in range(3):
        acc = per_chan(taps[m][:, 0]) * stream_grads[m]
        for j in range(1, tap_count):
            acc = acc + per_chan(taps[m][:, j]) * advance(stream_grads[m], j)
        pre_grads.append(acc)
        tap_cols.append(
            jnp.stack(
                [jnp.sum(stream_grads[m] * pres[m], axis=(0, 2))]
                + [
                    jnp.sum(stream_grads[m] * delayed(pres[m], j), axis=(0, 2))
                    for j in range(1, tap_count)
                ],
                axis=-1,
            )
        )
    return (jnp.stack(pre_grads, axis=1), grad_residues, grad_skip, jnp.stack(tap_cols))


def on_device(
    query_pre, key_pre, value_pre, grad_out, w_value, short_taps, residues, decay_rates, skip
):
    tap_count = short_taps.shape[2]
    owners = lax.axis_size("ctx")
    tokens_here, chans_here = query_pre.shape
    local_chans = chans_here // owners

    def to_owner_form(values_in):
        return jnp.transpose(values_in.reshape(tokens_here, owners, local_chans), (1, 2, 0))

    stacked_in = jnp.stack(
        [to_owner_form(query_pre), to_owner_form(key_pre), to_owner_form(value_pre), to_owner_form(grad_out)],
        axis=1,
    )
    gathered_in = lax.all_to_all(stacked_in, "ctx", split_axis=0, concat_axis=0, tiled=True)
    regrouped = tuple(gathered_in[:, i].astype(jnp.float32) for i in range(4))
    begin_at = lax.axis_index("ctx") * local_chans

    def own_rows(table):
        return lax.dynamic_slice_in_dim(table, begin_at, local_chans, 0)

    taps_here = jnp.transpose(own_rows(short_taps), (1, 0, 2))
    pre_grads, part_residues, part_skip, part_taps = blocked_backward(
        (regrouped[0], regrouped[1], regrouped[2]),
        regrouped[3],
        taps_here,
        own_rows(residues),
        own_rows(decay_rates),
        own_rows(skip),
    )
    rounded = pre_grads.astype(jnp.bfloat16)
    returned = lax.all_to_all(rounded, "ctx", split_axis=0, concat_axis=0, tiled=True)
    flat = jnp.transpose(returned, (1, 3, 0, 2)).reshape(3, tokens_here, chans_here)
    query_grad = flat[0]
    key_grad = flat[1]
    value_grad = flat[2]
    local_rows = part_residues.shape[0]
    packed = jnp.concatenate(
        [
            part_residues,
            part_skip[:, None],
            jnp.transpose(part_taps, (1, 0, 2)).reshape(local_rows, -1),
        ],
        axis=1,
    )
    spread = jnp.broadcast_to(packed[None], (owners,) + packed.shape)
    everyone = lax.all_to_all(spread, "ctx", split_axis=0, concat_axis=0, tiled=True)
    everyone = everyone.reshape(owners * local_rows, packed.shape[1])
    mode_count = part_residues.shape[1]
    d_residues = everyone[:, :mode_count]
    d_skip = everyone[:, mode_count]
    d_taps = everyone[:, mode_count + 1 :].reshape(-1, part_taps.shape[0], tap_count)
    partial_sum = lax.dot_general(
        value_grad, w_value, (((1,), (1,)), ((), ())), preferred_element_type=jnp.float32
    )
    narrowed = partial_sum.astype(jnp.bfloat16)
    groups = lax.axis_size("tp")
    here = lax.axis_index("tp")
    rows_each = narrowed.shape[0] // groups
    total = lax.dynamic_slice_in_dim(narrowed, here * rows_each, rows_each, 0).astype(jnp.float32)
    for shift in range(1, groups):
        outgoing = lax.dynamic_slice_in_dim(
            narrowed, lax.rem(here + shift, groups) * rows_each, rows_each, 0
        )
        incoming = lax.ppermute(
            outgoing, "tp", [(i, (i + shift) % groups) for i in range(groups)]
        )
        total = total + incoming.astype(jnp.float32)
    input_grad = total.astype(jnp.bfloat16)
    return (input_grad, query_grad, key_grad, d_residues, d_skip, d_taps)


def solution(mesh):
    in_specs = (
        P("ctx", "tp"),
        P("ctx", "tp"),
        P("ctx", "tp"),
        P("ctx", "tp"),
        P(None, "tp"),
        P("tp", None, None),
        P("tp", None),
        P("tp", None),
        P("tp"),
    )
    out_specs = (
        P(("ctx", "tp"), None),
        P("ctx", "tp"),
        P("ctx", "tp"),
        P("tp", None),
        P("tp"),
        P("tp", None, None),
    )
    return jax.shard_map(
        on_device, mesh=mesh, in_specs=in_specs, out_specs=out_specs, check_vma=False
    )
```

```python
import jax
import jax.numpy as jnp
from jax import lax
from jax.sharding import PartitionSpec as P

highest = lax.Precision.HIGHEST


def compose(earlier, later):
    return (earlier[0] * later[0], later[0] * earlier[1] + later[1])


def modal_states(signal, rate_table):
    channels, length = signal.shape
    mode_count = rate_table.shape[1]
    block_len = min(128, length)
    blocks = length // block_len
    offsets = jnp.arange(block_len, dtype=jnp.float32)
    growth = jnp.exp(rate_table[:, :, None] * offsets)
    shrink = jnp.exp(-rate_table[:, :, None] * offsets)
    lifted = signal.reshape(channels, 1, blocks, block_len) * growth[:, :, None, :]
    triangle = (offsets[None, :] <= offsets[:, None]).astype(jnp.float32)
    inside = (
        jnp.einsum("cnks,ts->cnkt", lifted, triangle, precision=highest) * shrink[:, :, None, :]
    )
    block_decay = jnp.exp(-rate_table * block_len)
    span_table = jnp.broadcast_to(block_decay[:, :, None], inside.shape[:3])
    factor, block_ends = lax.associative_scan(compose, (span_table, inside[..., -1]), axis=2)
    before = jnp.concatenate([jnp.zeros_like(block_ends[..., :1]), block_ends[..., :-1]], axis=2)
    carried_in = (
        jnp.exp(-rate_table[:, :, None] * (offsets + 1.0))[:, :, None, :] * before[..., None]
    )
    states = inside + carried_in
    return (states.reshape(channels, mode_count, length), block_ends[..., -1])


def short_forward(streams, tap_table, history):
    tap_count = tap_table.shape[-1]
    length = streams.shape[-1]
    extended = jnp.concatenate([history, streams], axis=-1)
    summed = jnp.zeros_like(streams)
    for tap_index in range(tap_count):
        begin_at = tap_count - 1 - tap_index
        summed = (
            summed
            + tap_table[..., tap_index : tap_index + 1]
            * extended[..., begin_at : begin_at + length]
        )
    return (summed, extended)


def short_backward(stream_grads, tap_table, future):
    tap_count = tap_table.shape[-1]
    length = stream_grads.shape[-1]
    extended = jnp.concatenate([stream_grads, future], axis=-1)
    summed = jnp.zeros_like(stream_grads)
    for tap_index in range(tap_count):
        summed = (
            summed
            + tap_table[..., tap_index : tap_index + 1]
            * extended[..., tap_index : tap_index + length]
        )
    return summed


def tap_grads(stream_grads, extended, tap_count):
    length = stream_grads.shape[-1]
    columns = []
    for tap_index in range(tap_count):
        begin_at = tap_count - 1 - tap_index
        columns.append(jnp.sum(stream_grads * extended[..., begin_at : begin_at + length], axis=-1))
    return jnp.stack(columns, axis=-1)


def blocked_backward(pres, cotangent, taps, residue_table, rate_table, skip_table):
    tap_count = taps.shape[-1]
    blocks, chans, block_len = cotangent.shape

    def delayed(values_in, amount):
        prev = jnp.pad(values_in[:-1], ((1, 0), (0, 0), (0, 0)))
        return jnp.concatenate(
            [prev[:, :, block_len - amount :], values_in[:, :, : block_len - amount]], axis=2
        )

    def advance(values_in, amount):
        nxt = jnp.pad(values_in[1:], ((0, 1), (0, 0), (0, 0)))
        return jnp.concatenate([values_in[:, :, amount:], nxt[:, :, :amount]], axis=2)

    def per_chan(column):
        return column[None, :, None]

    feats = []
    for m in range(3):
        acc = per_chan(taps[m][:, 0]) * pres[m]
        for j in range(1, tap_count):
            acc = acc + per_chan(taps[m][:, j]) * delayed(pres[m], j)
        feats.append(acc)
    query_feat, key_feat, value_feat = feats
    xb = key_feat * value_feat
    gb = cotangent * query_feat
    skip_b = per_chan(skip_table)

    rate = rate_table[:, :, None]
    offs = jnp.arange(block_len, dtype=jnp.float32)
    up = jnp.exp(-rate * offs)
    down = jnp.exp(rate * offs)
    tri = (offs[:, None] <= offs[None, :]).astype(jnp.float32)
    toeplitz = (
        jnp.einsum("cns,cnt->cst", residue_table[:, :, None] * down, up, precision=highest) * tri
    )

    idx = jnp.arange(blocks, dtype=jnp.float32)
    gap = idx[:, None] - 1.0 - idx[None, :]
    carry_mat = jnp.where(
        gap >= 0, jnp.exp(-rate[..., None] * block_len * jnp.maximum(gap, 0.0)), 0.0
    )

    conv_intra = jnp.einsum("kcs,cst->kct", xb, toeplitz, precision=highest)
    tail_w = jnp.exp(-rate * (block_len - 1 - offs))
    ends = jnp.einsum("kcs,cns->cnk", xb, tail_w, precision=highest)
    carried = jnp.sum(carry_mat * ends[:, :, None, :], axis=3)
    lead_w = residue_table[:, :, None] * jnp.exp(-rate * (offs + 1.0))
    conv_carry = jnp.einsum("cnk,cnt->kct", carried, lead_w, precision=highest)
    conv_out = conv_intra + conv_carry

    back_intra = jnp.einsum("kct,cst->kcs", gb, toeplitz, precision=highest)
    starts = jnp.einsum("kct,cnt->cnk", gb, up, precision=highest)
    later = jnp.sum(carry_mat * starts[:, :, :, None], axis=2)
    back_w = jnp.exp(-rate * (block_len - offs))
    back_carry = jnp.einsum(
        "cnk,cns->kcs", later, residue_table[:, :, None] * back_w, precision=highest
    )
    grad_mixed = back_intra + back_carry + skip_b * gb

    pairs = jnp.einsum("kcs,kct->cst", xb, gb, precision=highest) * tri
    paired = jnp.einsum("cst,cnt->cns", pairs, up, precision=highest)
    res_intra = jnp.sum(paired * down, axis=2)
    lead_sums = jnp.einsum("kcs,cns->cnk", xb, back_w, precision=highest)
    grad_residues = res_intra + jnp.sum(later * lead_sums, axis=2)
    grad_skip = jnp.sum(gb * xb, axis=(0, 2))

    grad_query = cotangent * (conv_out + skip_b * xb)
    stream_grads = (grad_query, grad_mixed * value_feat, grad_mixed * key_feat)
    pre_grads = []
    tap_cols = []
    for m in range(3):
        acc = per_chan(taps[m][:, 0]) * stream_grads[m]
        for j in range(1, tap_count):
            acc = acc + per_chan(taps[m][:, j]) * advance(stream_grads[m], j)
        pre_grads.append(acc)
        tap_cols.append(
            jnp.stack(
                [jnp.sum(stream_grads[m] * pres[m], axis=(0, 2))]
                + [
                    jnp.sum(stream_grads[m] * delayed(pres[m], j), axis=(0, 2))
                    for j in range(1, tap_count)
                ],
                axis=-1,
            )
        )
    return (jnp.stack(pre_grads, axis=1), grad_residues, grad_skip, jnp.stack(tap_cols))


def on_device(
    query_pre, key_pre, value_pre, grad_out, w_value, short_taps, residues, decay_rates, skip
):
    tap_count = short_taps.shape[2]
    owners = lax.axis_size("ctx")
    tokens_here, chans_here = query_pre.shape
    local_chans = chans_here // owners

    def to_owner_form(values_in):
        return jnp.transpose(values_in.reshape(tokens_here, owners, local_chans), (1, 2, 0))

    stacked_in = jnp.stack(
        [to_owner_form(query_pre), to_owner_form(key_pre), to_owner_form(value_pre), to_owner_form(grad_out)],
        axis=1,
    )
    gathered_in = lax.all_to_all(stacked_in, "ctx", split_axis=0, concat_axis=0, tiled=True)
    regrouped = tuple(gathered_in[:, i].astype(jnp.float32) for i in range(4))
    begin_at = lax.axis_index("ctx") * local_chans

    def own_rows(table):
        return lax.dynamic_slice_in_dim(table, begin_at, local_chans, 0)

    taps_here = jnp.transpose(own_rows(short_taps), (1, 0, 2))
    pre_grads, part_residues, part_skip, part_taps = blocked_backward(
        (regrouped[0], regrouped[1], regrouped[2]),
        regrouped[3],
        taps_here,
        own_rows(residues),
        own_rows(decay_rates),
        own_rows(skip),
    )
    rounded = pre_grads.astype(jnp.bfloat16)
    returned = lax.all_to_all(rounded, "ctx", split_axis=0, concat_axis=0, tiled=True)
    flat = jnp.transpose(returned, (1, 3, 0, 2)).reshape(3, tokens_here, chans_here)
    query_grad = flat[0]
    key_grad = flat[1]
    value_grad = flat[2]
    local_rows = part_residues.shape[0]
    packed = jnp.concatenate(
        [
            part_residues,
            part_skip[:, None],
            jnp.transpose(part_taps, (1, 0, 2)).reshape(local_rows, -1),
        ],
        axis=1,
    )
    spread = jnp.broadcast_to(packed[None], (owners,) + packed.shape)
    query_grad, key_grad, spread = lax.optimization_barrier((query_grad, key_grad, spread))
    everyone = lax.all_to_all(spread, "ctx", split_axis=0, concat_axis=0, tiled=True)
    everyone = everyone.reshape(owners * local_rows, packed.shape[1])
    mode_count = part_residues.shape[1]
    d_residues = everyone[:, :mode_count]
    d_skip = everyone[:, mode_count]
    d_taps = everyone[:, mode_count + 1 :].reshape(-1, part_taps.shape[0], tap_count)
    partial_sum = lax.dot_general(
        value_grad, w_value, (((1,), (1,)), ((), ())), preferred_element_type=jnp.float32
    )
    narrowed = partial_sum.astype(jnp.bfloat16)
    groups = lax.axis_size("tp")
    here = lax.axis_index("tp")
    rows_each = narrowed.shape[0] // groups
    total = lax.dynamic_slice_in_dim(narrowed, here * rows_each, rows_each, 0).astype(jnp.float32)
    for shift in range(1, groups):
        outgoing = lax.dynamic_slice_in_dim(
            narrowed, lax.rem(here + shift, groups) * rows_each, rows_each, 0
        )
        incoming = lax.ppermute(
            outgoing, "tp", [(i, (i + shift) % groups) for i in range(groups)]
        )
        total = total + incoming.astype(jnp.float32)
    input_grad = total.astype(jnp.bfloat16)
    return (input_grad, query_grad, key_grad, d_residues, d_skip, d_taps)


def solution(mesh):
    in_specs = (
        P("ctx", "tp"),
        P("ctx", "tp"),
        P("ctx", "tp"),
        P("ctx", "tp"),
        P(None, "tp"),
        P("tp", None, None),
        P("tp", None),
        P("tp", None),
        P("tp"),
    )
    out_specs = (
        P(("ctx", "tp"), None),
        P("ctx", "tp"),
        P("ctx", "tp"),
        P("tp", None),
        P("tp"),
        P("tp", None, None),
    )
    return jax.shard_map(
        on_device, mesh=mesh, in_specs=in_specs, out_specs=out_specs, check_vma=False
    )
```

```python
import jax
import jax.numpy as jnp
from jax import lax
from jax.sharding import PartitionSpec as P

highest = lax.Precision.HIGHEST


def compose(earlier, later):
    return (earlier[0] * later[0], later[0] * earlier[1] + later[1])


def modal_states(signal, rate_table):
    channels, length = signal.shape
    mode_count = rate_table.shape[1]
    block_len = min(128, length)
    blocks = length // block_len
    offsets = jnp.arange(block_len, dtype=jnp.float32)
    growth = jnp.exp(rate_table[:, :, None] * offsets)
    shrink = jnp.exp(-rate_table[:, :, None] * offsets)
    lifted = signal.reshape(channels, 1, blocks, block_len) * growth[:, :, None, :]
    triangle = (offsets[None, :] <= offsets[:, None]).astype(jnp.float32)
    inside = (
        jnp.einsum("cnks,ts->cnkt", lifted, triangle, precision=highest) * shrink[:, :, None, :]
    )
    block_decay = jnp.exp(-rate_table * block_len)
    span_table = jnp.broadcast_to(block_decay[:, :, None], inside.shape[:3])
    factor, block_ends = lax.associative_scan(compose, (span_table, inside[..., -1]), axis=2)
    before = jnp.concatenate([jnp.zeros_like(block_ends[..., :1]), block_ends[..., :-1]], axis=2)
    carried_in = (
        jnp.exp(-rate_table[:, :, None] * (offsets + 1.0))[:, :, None, :] * before[..., None]
    )
    states = inside + carried_in
    return (states.reshape(channels, mode_count, length), block_ends[..., -1])


def short_forward(streams, tap_table, history):
    tap_count = tap_table.shape[-1]
    length = streams.shape[-1]
    extended = jnp.concatenate([history, streams], axis=-1)
    summed = jnp.zeros_like(streams)
    for tap_index in range(tap_count):
        begin_at = tap_count - 1 - tap_index
        summed = (
            summed
            + tap_table[..., tap_index : tap_index + 1]
            * extended[..., begin_at : begin_at + length]
        )
    return (summed, extended)


def short_backward(stream_grads, tap_table, future):
    tap_count = tap_table.shape[-1]
    length = stream_grads.shape[-1]
    extended = jnp.concatenate([stream_grads, future], axis=-1)
    summed = jnp.zeros_like(stream_grads)
    for tap_index in range(tap_count):
        summed = (
            summed
            + tap_table[..., tap_index : tap_index + 1]
            * extended[..., tap_index : tap_index + length]
        )
    return summed


def tap_grads(stream_grads, extended, tap_count):
    length = stream_grads.shape[-1]
    columns = []
    for tap_index in range(tap_count):
        begin_at = tap_count - 1 - tap_index
        columns.append(jnp.sum(stream_grads * extended[..., begin_at : begin_at + length], axis=-1))
    return jnp.stack(columns, axis=-1)


def blocked_backward(pres, cotangent, taps, residue_table, rate_table, skip_table):
    tap_count = taps.shape[-1]
    blocks, chans, block_len = cotangent.shape

    def delayed(values_in, amount):
        prev = jnp.pad(values_in[:-1], ((1, 0), (0, 0), (0, 0)))
        return jnp.concatenate(
            [prev[:, :, block_len - amount :], values_in[:, :, : block_len - amount]], axis=2
        )

    def advance(values_in, amount):
        nxt = jnp.pad(values_in[1:], ((0, 1), (0, 0), (0, 0)))
        return jnp.concatenate([values_in[:, :, amount:], nxt[:, :, :amount]], axis=2)

    def per_chan(column):
        return column[None, :, None]

    feats = []
    for m in range(3):
        acc = per_chan(taps[m][:, 0]) * pres[m]
        for j in range(1, tap_count):
            acc = acc + per_chan(taps[m][:, j]) * delayed(pres[m], j)
        feats.append(acc)
    query_feat, key_feat, value_feat = feats
    xb = key_feat * value_feat
    gb = cotangent * query_feat
    skip_b = per_chan(skip_table)

    rate = rate_table[:, :, None]
    offs = jnp.arange(block_len, dtype=jnp.float32)
    up = jnp.exp(-rate * offs)
    down = jnp.exp(rate * offs)
    tri = (offs[:, None] <= offs[None, :]).astype(jnp.float32)
    toeplitz = (
        jnp.einsum("cns,cnt->cst", residue_table[:, :, None] * down, up, precision=highest) * tri
    )

    idx = jnp.arange(blocks, dtype=jnp.float32)
    gap = idx[:, None] - 1.0 - idx[None, :]
    carry_mat = jnp.where(
        gap >= 0, jnp.exp(-rate[..., None] * block_len * jnp.maximum(gap, 0.0)), 0.0
    )

    conv_intra = jnp.einsum("kcs,cst->kct", xb, toeplitz, precision=highest)
    tail_w = jnp.exp(-rate * (block_len - 1 - offs))
    ends = jnp.einsum("kcs,cns->cnk", xb, tail_w, precision=highest)
    carried = jnp.sum(carry_mat * ends[:, :, None, :], axis=3)
    lead_w = residue_table[:, :, None] * jnp.exp(-rate * (offs + 1.0))
    conv_carry = jnp.einsum("cnk,cnt->kct", carried, lead_w, precision=highest)
    conv_out = conv_intra + conv_carry

    back_intra = jnp.einsum("kct,cst->kcs", gb, toeplitz, precision=highest)
    starts = jnp.einsum("kct,cnt->cnk", gb, up, precision=highest)
    later = jnp.sum(carry_mat * starts[:, :, :, None], axis=2)
    back_w = jnp.exp(-rate * (block_len - offs))
    back_carry = jnp.einsum(
        "cnk,cns->kcs", later, residue_table[:, :, None] * back_w, precision=highest
    )
    grad_mixed = back_intra + back_carry + skip_b * gb

    pairs = jnp.einsum("kcs,kct->cst", xb, gb, precision=highest) * tri
    paired = jnp.einsum("cst,cnt->cns", pairs, up, precision=highest)
    res_intra = jnp.sum(paired * down, axis=2)
    lead_sums = jnp.einsum("kcs,cns->cnk", xb, back_w, precision=highest)
    grad_residues = res_intra + jnp.sum(later * lead_sums, axis=2)
    grad_skip = jnp.sum(gb * xb, axis=(0, 2))

    grad_query = cotangent * (conv_out + skip_b * xb)
    stream_grads = (grad_query, grad_mixed * value_feat, grad_mixed * key_feat)
    pre_grads = []
    tap_cols = []
    for m in range(3):
        acc = per_chan(taps[m][:, 0]) * stream_grads[m]
        for j in range(1, tap_count):
            acc = acc + per_chan(taps[m][:, j]) * advance(stream_grads[m], j)
        pre_grads.append(acc)
        tap_cols.append(
            jnp.stack(
                [jnp.sum(stream_grads[m] * pres[m], axis=(0, 2))]
                + [
                    jnp.sum(stream_grads[m] * delayed(pres[m], j), axis=(0, 2))
                    for j in range(1, tap_count)
                ],
                axis=-1,
            )
        )
    return (jnp.stack(pre_grads, axis=1), grad_residues, grad_skip, jnp.stack(tap_cols))


def on_device(
    query_pre, key_pre, value_pre, grad_out, w_value, short_taps, residues, decay_rates, skip
):
    tap_count = short_taps.shape[2]
    owners = lax.axis_size("ctx")
    tokens_here, chans_here = query_pre.shape
    local_chans = chans_here // owners

    def to_owner_form(values_in):
        return jnp.transpose(values_in.reshape(tokens_here, owners, local_chans), (1, 2, 0))

    stacked_in = jnp.stack(
        [to_owner_form(query_pre), to_owner_form(key_pre), to_owner_form(value_pre), to_owner_form(grad_out)],
        axis=1,
    )
    gathered_in = lax.all_to_all(stacked_in, "ctx", split_axis=0, concat_axis=0, tiled=True)
    regrouped = tuple(gathered_in[:, i].astype(jnp.float32) for i in range(4))
    begin_at = lax.axis_index("ctx") * local_chans

    def own_rows(table):
        return lax.dynamic_slice_in_dim(table, begin_at, local_chans, 0)

    taps_here = jnp.transpose(own_rows(short_taps), (1, 0, 2))
    pre_grads, part_residues, part_skip, part_taps = blocked_backward(
        (regrouped[0], regrouped[1], regrouped[2]),
        regrouped[3],
        taps_here,
        own_rows(residues),
        own_rows(decay_rates),
        own_rows(skip),
    )
    rounded = pre_grads.astype(jnp.bfloat16)
    returned = lax.all_to_all(rounded, "ctx", split_axis=0, concat_axis=0, tiled=True)
    flat = jnp.transpose(returned, (1, 3, 0, 2)).reshape(3, tokens_here, chans_here)
    query_grad = flat[0]
    key_grad = flat[1]
    value_grad = flat[2]
    local_rows = part_residues.shape[0]
    packed = jnp.concatenate(
        [
            part_residues,
            part_skip[:, None],
            jnp.transpose(part_taps, (1, 0, 2)).reshape(local_rows, -1),
        ],
        axis=1,
    )
    spread = jnp.broadcast_to(packed[None], (owners,) + packed.shape)
    query_grad, key_grad, spread = lax.optimization_barrier((query_grad, key_grad, spread))
    everyone = lax.all_to_all(spread, "ctx", split_axis=0, concat_axis=0, tiled=True)
    everyone = everyone.reshape(owners * local_rows, packed.shape[1])
    mode_count = part_residues.shape[1]
    d_residues = everyone[:, :mode_count]
    d_skip = everyone[:, mode_count]
    d_taps = everyone[:, mode_count + 1 :].reshape(-1, part_taps.shape[0], tap_count)
    groups = lax.axis_size("tp")
    here = lax.axis_index("tp")
    rows_each = value_grad.shape[0] // groups
    rolled = jnp.roll(value_grad.reshape(groups, rows_each, -1), -here, axis=0)
    partial_sum = lax.dot_general(
        rolled.reshape(value_grad.shape), w_value, (((1,), (1,)), ((), ())),
        preferred_element_type=jnp.float32,
    )
    narrowed = partial_sum.astype(jnp.bfloat16).reshape(groups, rows_each, -1)
    total = narrowed[0].astype(jnp.float32)
    for shift in range(1, groups):
        incoming = lax.ppermute(
            narrowed[shift], "tp", [(i, (i + shift) % groups) for i in range(groups)]
        )
        total = total + incoming.astype(jnp.float32)
    input_grad = total.astype(jnp.bfloat16)
    return (input_grad, query_grad, key_grad, d_residues, d_skip, d_taps)


def solution(mesh):
    in_specs = (
        P("ctx", "tp"),
        P("ctx", "tp"),
        P("ctx", "tp"),
        P("ctx", "tp"),
        P(None, "tp"),
        P("tp", None, None),
        P("tp", None),
        P("tp", None),
        P("tp"),
    )
    out_specs = (
        P(("ctx", "tp"), None),
        P("ctx", "tp"),
        P("ctx", "tp"),
        P("tp", None),
        P("tp"),
        P("tp", None, None),
    )
    return jax.shard_map(
        on_device, mesh=mesh, in_specs=in_specs, out_specs=out_specs, check_vma=False
    )
```

```python
import jax
import jax.numpy as jnp
from jax import lax
from jax.sharding import PartitionSpec as P

highest = lax.Precision.HIGHEST


def compose(earlier, later):
    return (earlier[0] * later[0], later[0] * earlier[1] + later[1])


def modal_states(signal, rate_table):
    channels, length = signal.shape
    mode_count = rate_table.shape[1]
    block_len = min(128, length)
    blocks = length // block_len
    offsets = jnp.arange(block_len, dtype=jnp.float32)
    growth = jnp.exp(rate_table[:, :, None] * offsets)
    shrink = jnp.exp(-rate_table[:, :, None] * offsets)
    lifted = signal.reshape(channels, 1, blocks, block_len) * growth[:, :, None, :]
    triangle = (offsets[None, :] <= offsets[:, None]).astype(jnp.float32)
    inside = (
        jnp.einsum("cnks,ts->cnkt", lifted, triangle, precision=highest) * shrink[:, :, None, :]
    )
    block_decay = jnp.exp(-rate_table * block_len)
    span_table = jnp.broadcast_to(block_decay[:, :, None], inside.shape[:3])
    factor, block_ends = lax.associative_scan(compose, (span_table, inside[..., -1]), axis=2)
    before = jnp.concatenate([jnp.zeros_like(block_ends[..., :1]), block_ends[..., :-1]], axis=2)
    carried_in = (
        jnp.exp(-rate_table[:, :, None] * (offsets + 1.0))[:, :, None, :] * before[..., None]
    )
    states = inside + carried_in
    return (states.reshape(channels, mode_count, length), block_ends[..., -1])


def short_forward(streams, tap_table, history):
    tap_count = tap_table.shape[-1]
    length = streams.shape[-1]
    extended = jnp.concatenate([history, streams], axis=-1)
    summed = jnp.zeros_like(streams)
    for tap_index in range(tap_count):
        begin_at = tap_count - 1 - tap_index
        summed = (
            summed
            + tap_table[..., tap_index : tap_index + 1]
            * extended[..., begin_at : begin_at + length]
        )
    return (summed, extended)


def short_backward(stream_grads, tap_table, future):
    tap_count = tap_table.shape[-1]
    length = stream_grads.shape[-1]
    extended = jnp.concatenate([stream_grads, future], axis=-1)
    summed = jnp.zeros_like(stream_grads)
    for tap_index in range(tap_count):
        summed = (
            summed
            + tap_table[..., tap_index : tap_index + 1]
            * extended[..., tap_index : tap_index + length]
        )
    return summed


def tap_grads(stream_grads, extended, tap_count):
    length = stream_grads.shape[-1]
    columns = []
    for tap_index in range(tap_count):
        begin_at = tap_count - 1 - tap_index
        columns.append(jnp.sum(stream_grads * extended[..., begin_at : begin_at + length], axis=-1))
    return jnp.stack(columns, axis=-1)


def blocked_backward(pres, cotangent, taps, residue_table, rate_table, skip_table):
    tap_count = taps.shape[-1]
    blocks, chans, block_len = cotangent.shape

    def delayed(values_in, amount):
        prev = jnp.pad(values_in[:-1], ((1, 0), (0, 0), (0, 0)))
        return jnp.concatenate(
            [prev[:, :, block_len - amount :], values_in[:, :, : block_len - amount]], axis=2
        )

    def advance(values_in, amount):
        nxt = jnp.pad(values_in[1:], ((0, 1), (0, 0), (0, 0)))
        return jnp.concatenate([values_in[:, :, amount:], nxt[:, :, :amount]], axis=2)

    def per_chan(column):
        return column[None, :, None]

    feats = []
    for m in range(3):
        acc = per_chan(taps[m][:, 0]) * pres[m]
        for j in range(1, tap_count):
            acc = acc + per_chan(taps[m][:, j]) * delayed(pres[m], j)
        feats.append(acc)
    query_feat, key_feat, value_feat = feats
    xb = key_feat * value_feat
    gb = cotangent * query_feat
    skip_b = per_chan(skip_table)

    rate = rate_table[:, :, None]
    offs = jnp.arange(block_len, dtype=jnp.float32)
    up = jnp.exp(-rate * offs)
    down = jnp.exp(rate * offs)
    tri = (offs[:, None] <= offs[None, :]).astype(jnp.float32)
    toeplitz = (
        jnp.einsum("cns,cnt->cst", residue_table[:, :, None] * down, up, precision=highest) * tri
    )

    idx = jnp.arange(blocks, dtype=jnp.float32)
    gap = idx[:, None] - 1.0 - idx[None, :]
    rate_flat = rate_table.reshape(-1)
    modes = rate_table.shape[1]
    carry_mat = jnp.where(
        gap[..., None] >= 0,
        jnp.exp(-rate_flat * block_len * jnp.maximum(gap, 0.0)[..., None]),
        0.0,
    )

    conv_intra = jnp.einsum("kcs,cst->kct", xb, toeplitz, precision=highest)
    tail_w = jnp.exp(-rate * (block_len - 1 - offs))
    ends = jnp.einsum("kcs,cns->kcn", xb, tail_w, precision=highest).reshape(blocks, -1)
    carried = jnp.sum(carry_mat * ends[None, :, :], axis=1).reshape(blocks, chans, modes)
    lead_w = residue_table[:, :, None] * jnp.exp(-rate * (offs + 1.0))
    conv_carry = jnp.einsum("kcn,cnt->kct", carried, lead_w, precision=highest)
    conv_out = conv_intra + conv_carry

    back_intra = jnp.einsum("kct,cst->kcs", gb, toeplitz, precision=highest)
    starts = jnp.einsum("kct,cnt->kcn", gb, up, precision=highest).reshape(blocks, -1)
    later = jnp.sum(carry_mat * starts[:, None, :], axis=0).reshape(blocks, chans, modes)
    back_w = jnp.exp(-rate * (block_len - offs))
    back_carry = jnp.einsum(
        "kcn,cns->kcs", later, residue_table[:, :, None] * back_w, precision=highest
    )
    grad_mixed = back_intra + back_carry + skip_b * gb

    pairs = jnp.einsum("kcs,kct->cst", xb, gb, precision=highest) * tri
    paired = jnp.einsum("cst,cnt->cns", pairs, up, precision=highest)
    res_intra = jnp.sum(paired * down, axis=2)
    lead_sums = jnp.einsum("kcs,cns->kcn", xb, back_w, precision=highest)
    grad_residues = res_intra + jnp.sum(later * lead_sums, axis=0)
    grad_skip = jnp.sum(gb * xb, axis=(0, 2))

    grad_query = cotangent * (conv_out + skip_b * xb)
    stream_grads = (grad_query, grad_mixed * value_feat, grad_mixed * key_feat)
    pre_grads = []
    tap_cols = []
    for m in range(3):
        acc = per_chan(taps[m][:, 0]) * stream_grads[m]
        for j in range(1, tap_count):
            acc = acc + per_chan(taps[m][:, j]) * advance(stream_grads[m], j)
        pre_grads.append(acc)
        tap_cols.append(
            jnp.stack(
                [jnp.sum(stream_grads[m] * pres[m], axis=(0, 2))]
                + [
                    jnp.sum(stream_grads[m] * delayed(pres[m], j), axis=(0, 2))
                    for j in range(1, tap_count)
                ],
                axis=-1,
            )
        )
    return (jnp.stack(pre_grads, axis=1), grad_residues, grad_skip, jnp.stack(tap_cols))


def on_device(
    query_pre, key_pre, value_pre, grad_out, w_value, short_taps, residues, decay_rates, skip
):
    tap_count = short_taps.shape[2]
    owners = lax.axis_size("ctx")
    tokens_here, chans_here = query_pre.shape
    local_chans = chans_here // owners

    def to_owner_form(values_in):
        return jnp.transpose(values_in.reshape(tokens_here, owners, local_chans), (1, 2, 0))

    stacked_in = jnp.stack(
        [to_owner_form(query_pre), to_owner_form(key_pre), to_owner_form(value_pre), to_owner_form(grad_out)],
        axis=1,
    )
    gathered_in = lax.all_to_all(stacked_in, "ctx", split_axis=0, concat_axis=0, tiled=True)
    regrouped = tuple(gathered_in[:, i].astype(jnp.float32) for i in range(4))
    begin_at = lax.axis_index("ctx") * local_chans

    def own_rows(table):
        return lax.dynamic_slice_in_dim(table, begin_at, local_chans, 0)

    taps_here = jnp.transpose(own_rows(short_taps), (1, 0, 2))
    pre_grads, part_residues, part_skip, part_taps = blocked_backward(
        (regrouped[0], regrouped[1], regrouped[2]),
        regrouped[3],
        taps_here,
        own_rows(residues),
        own_rows(decay_rates),
        own_rows(skip),
    )
    rounded = pre_grads.astype(jnp.bfloat16)
    returned = lax.all_to_all(rounded, "ctx", split_axis=0, concat_axis=0, tiled=True)
    flat = jnp.transpose(returned, (1, 3, 0, 2)).reshape(3, tokens_here, chans_here)
    query_grad = flat[0]
    key_grad = flat[1]
    value_grad = flat[2]
    local_rows = part_residues.shape[0]
    packed = jnp.concatenate(
        [
            part_residues,
            part_skip[:, None],
            jnp.transpose(part_taps, (1, 0, 2)).reshape(local_rows, -1),
        ],
        axis=1,
    )
    spread = jnp.broadcast_to(packed[None], (owners,) + packed.shape)
    query_grad, key_grad, spread = lax.optimization_barrier((query_grad, key_grad, spread))
    everyone = lax.all_to_all(spread, "ctx", split_axis=0, concat_axis=0, tiled=True)
    everyone = everyone.reshape(owners * local_rows, packed.shape[1])
    mode_count = part_residues.shape[1]
    d_residues = everyone[:, :mode_count]
    d_skip = everyone[:, mode_count]
    d_taps = everyone[:, mode_count + 1 :].reshape(-1, part_taps.shape[0], tap_count)
    groups = lax.axis_size("tp")
    here = lax.axis_index("tp")
    rows_each = value_grad.shape[0] // groups
    rolled = jnp.roll(value_grad.reshape(groups, rows_each, -1), -here, axis=0)
    partial_sum = lax.dot_general(
        rolled.reshape(value_grad.shape), w_value, (((1,), (1,)), ((), ())),
        preferred_element_type=jnp.float32,
    )
    narrowed = partial_sum.astype(jnp.bfloat16).reshape(groups, rows_each, -1)
    total = narrowed[0].astype(jnp.float32)
    for shift in range(1, groups):
        incoming = lax.ppermute(
            narrowed[shift], "tp", [(i, (i + shift) % groups) for i in range(groups)]
        )
        total = total + incoming.astype(jnp.float32)
    input_grad = total.astype(jnp.bfloat16)
    return (input_grad, query_grad, key_grad, d_residues, d_skip, d_taps)


def solution(mesh):
    in_specs = (
        P("ctx", "tp"),
        P("ctx", "tp"),
        P("ctx", "tp"),
        P("ctx", "tp"),
        P(None, "tp"),
        P("tp", None, None),
        P("tp", None),
        P("tp", None),
        P("tp"),
    )
    out_specs = (
        P(("ctx", "tp"), None),
        P("ctx", "tp"),
        P("ctx", "tp"),
        P("tp", None),
        P("tp"),
        P("tp", None, None),
    )
    return jax.shard_map(
        on_device, mesh=mesh, in_specs=in_specs, out_specs=out_specs, check_vma=False
    )
```

```python
import jax
import jax.numpy as jnp
from jax import lax
from jax.sharding import PartitionSpec as P

highest = lax.Precision.HIGHEST


def compose(earlier, later):
    return (earlier[0] * later[0], later[0] * earlier[1] + later[1])


def modal_states(signal, rate_table):
    channels, length = signal.shape
    mode_count = rate_table.shape[1]
    block_len = min(128, length)
    blocks = length // block_len
    offsets = jnp.arange(block_len, dtype=jnp.float32)
    growth = jnp.exp(rate_table[:, :, None] * offsets)
    shrink = jnp.exp(-rate_table[:, :, None] * offsets)
    lifted = signal.reshape(channels, 1, blocks, block_len) * growth[:, :, None, :]
    triangle = (offsets[None, :] <= offsets[:, None]).astype(jnp.float32)
    inside = (
        jnp.einsum("cnks,ts->cnkt", lifted, triangle, precision=highest) * shrink[:, :, None, :]
    )
    block_decay = jnp.exp(-rate_table * block_len)
    span_table = jnp.broadcast_to(block_decay[:, :, None], inside.shape[:3])
    factor, block_ends = lax.associative_scan(compose, (span_table, inside[..., -1]), axis=2)
    before = jnp.concatenate([jnp.zeros_like(block_ends[..., :1]), block_ends[..., :-1]], axis=2)
    carried_in = (
        jnp.exp(-rate_table[:, :, None] * (offsets + 1.0))[:, :, None, :] * before[..., None]
    )
    states = inside + carried_in
    return (states.reshape(channels, mode_count, length), block_ends[..., -1])


def short_forward(streams, tap_table, history):
    tap_count = tap_table.shape[-1]
    length = streams.shape[-1]
    extended = jnp.concatenate([history, streams], axis=-1)
    summed = jnp.zeros_like(streams)
    for tap_index in range(tap_count):
        begin_at = tap_count - 1 - tap_index
        summed = (
            summed
            + tap_table[..., tap_index : tap_index + 1]
            * extended[..., begin_at : begin_at + length]
        )
    return (summed, extended)


def short_backward(stream_grads, tap_table, future):
    tap_count = tap_table.shape[-1]
    length = stream_grads.shape[-1]
    extended = jnp.concatenate([stream_grads, future], axis=-1)
    summed = jnp.zeros_like(stream_grads)
    for tap_index in range(tap_count):
        summed = (
            summed
            + tap_table[..., tap_index : tap_index + 1]
            * extended[..., tap_index : tap_index + length]
        )
    return summed


def tap_grads(stream_grads, extended, tap_count):
    length = stream_grads.shape[-1]
    columns = []
    for tap_index in range(tap_count):
        begin_at = tap_count - 1 - tap_index
        columns.append(jnp.sum(stream_grads * extended[..., begin_at : begin_at + length], axis=-1))
    return jnp.stack(columns, axis=-1)


def blocked_backward(pres, cotangent, taps, residue_table, rate_table, skip_table):
    tap_count = taps.shape[-1]
    blocks, chans, block_len = cotangent.shape

    def delayed(values_in, amount):
        prev = jnp.pad(values_in[:-1], ((1, 0), (0, 0), (0, 0)))
        return jnp.concatenate(
            [prev[:, :, block_len - amount :], values_in[:, :, : block_len - amount]], axis=2
        )

    def advance(values_in, amount):
        nxt = jnp.pad(values_in[1:], ((0, 1), (0, 0), (0, 0)))
        return jnp.concatenate([values_in[:, :, amount:], nxt[:, :, :amount]], axis=2)

    def per_chan(column):
        return column[None, :, None]

    feats = []
    for m in range(3):
        acc = per_chan(taps[m][:, 0]) * pres[m]
        for j in range(1, tap_count):
            acc = acc + per_chan(taps[m][:, j]) * delayed(pres[m], j)
        feats.append(acc)
    query_feat, key_feat, value_feat = feats
    xb = key_feat * value_feat
    gb = cotangent * query_feat
    skip_b = per_chan(skip_table)

    rate = rate_table[:, :, None]
    offs = jnp.arange(block_len, dtype=jnp.float32)
    up = jnp.exp(-rate * offs)
    down = jnp.exp(rate * offs)
    tri = (offs[:, None] <= offs[None, :]).astype(jnp.float32)
    toeplitz = (
        jnp.einsum("cns,cnt->cst", residue_table[:, :, None] * down, up, precision=highest) * tri
    )

    idx = jnp.arange(blocks, dtype=jnp.float32)
    gap = idx[:, None] - 1.0 - idx[None, :]
    carry_mat = jnp.where(
        gap >= 0, jnp.exp(-rate[..., None] * block_len * jnp.maximum(gap, 0.0)), 0.0
    )

    conv_intra = jnp.einsum("kcs,cst->kct", xb, toeplitz, precision=highest)
    tail_w = jnp.exp(-rate * (block_len - 1 - offs))
    ends = jnp.einsum("kcs,cns->cnk", xb, tail_w, precision=highest)
    carried = jnp.sum(carry_mat * ends[:, :, None, :], axis=3)
    lead_w = residue_table[:, :, None] * jnp.exp(-rate * (offs + 1.0))
    conv_carry = jnp.einsum("cnk,cnt->kct", carried, lead_w, precision=highest)
    conv_out = conv_intra + conv_carry

    back_intra = jnp.einsum("kct,cst->kcs", gb, toeplitz, precision=highest)
    starts = jnp.einsum("kct,cnt->cnk", gb, up, precision=highest)
    later = jnp.sum(carry_mat * starts[:, :, :, None], axis=2)
    back_w = jnp.exp(-rate * (block_len - offs))
    back_carry = jnp.einsum(
        "cnk,cns->kcs", later, residue_table[:, :, None] * back_w, precision=highest
    )
    grad_mixed = back_intra + back_carry + skip_b * gb

    pairs = jnp.einsum("kcs,kct->cst", xb, gb, precision=highest) * tri
    paired = jnp.einsum("cst,cnt->cns", pairs, up, precision=highest)
    res_intra = jnp.sum(paired * down, axis=2)
    lead_sums = jnp.einsum("kcs,cns->cnk", xb, back_w, precision=highest)
    grad_residues = res_intra + jnp.sum(later * lead_sums, axis=2)
    grad_skip = jnp.sum(gb * xb, axis=(0, 2))

    grad_query = cotangent * (conv_out + skip_b * xb)
    stream_grads = (grad_query, grad_mixed * value_feat, grad_mixed * key_feat)
    pre_grads = []
    tap_cols = []
    for m in range(3):
        acc = per_chan(taps[m][:, 0]) * stream_grads[m]
        for j in range(1, tap_count):
            acc = acc + per_chan(taps[m][:, j]) * advance(stream_grads[m], j)
        pre_grads.append(acc)
        tap_cols.append(
            jnp.stack(
                [jnp.sum(stream_grads[m] * pres[m], axis=(0, 2))]
                + [
                    jnp.sum(stream_grads[m] * delayed(pres[m], j), axis=(0, 2))
                    for j in range(1, tap_count)
                ],
                axis=-1,
            )
        )
    return (jnp.stack(pre_grads, axis=1), grad_residues, grad_skip, jnp.stack(tap_cols))


def on_device(
    query_pre, key_pre, value_pre, grad_out, w_value, short_taps, residues, decay_rates, skip
):
    tap_count = short_taps.shape[2]
    owners = lax.axis_size("ctx")
    tokens_here, chans_here = query_pre.shape
    local_chans = chans_here // owners

    def to_owner_form(values_in):
        return jnp.transpose(values_in.reshape(tokens_here, owners, local_chans), (1, 2, 0))

    stacked_in = jnp.stack(
        [to_owner_form(query_pre), to_owner_form(key_pre), to_owner_form(value_pre), to_owner_form(grad_out)],
        axis=1,
    )
    gathered_in = lax.all_to_all(stacked_in, "ctx", split_axis=0, concat_axis=0, tiled=True)
    regrouped = tuple(gathered_in[:, i].astype(jnp.float32) for i in range(4))
    begin_at = lax.axis_index("ctx") * local_chans

    def own_rows(table):
        return lax.dynamic_slice_in_dim(table, begin_at, local_chans, 0)

    taps_here = jnp.transpose(own_rows(short_taps), (1, 0, 2))
    pre_grads, part_residues, part_skip, part_taps = blocked_backward(
        (regrouped[0], regrouped[1], regrouped[2]),
        regrouped[3],
        taps_here,
        own_rows(residues),
        own_rows(decay_rates),
        own_rows(skip),
    )
    rounded = pre_grads.astype(jnp.bfloat16)
    returned = lax.all_to_all(rounded, "ctx", split_axis=0, concat_axis=0, tiled=True)
    flat = jnp.transpose(returned, (1, 3, 0, 2)).reshape(3, tokens_here, chans_here)
    query_grad = flat[0]
    key_grad = flat[1]
    value_grad = flat[2]
    local_rows = part_residues.shape[0]
    packed = jnp.concatenate(
        [
            part_residues,
            part_skip[:, None],
            jnp.transpose(part_taps, (1, 0, 2)).reshape(local_rows, -1),
        ],
        axis=1,
    )
    packed_len = packed.shape[0] * packed.shape[1]
    lane_rows = -(-packed_len // 128)
    tiled_pack = jnp.pad(packed.reshape(-1), (0, lane_rows * 128 - packed_len)).reshape(lane_rows, 128)
    spread = jnp.broadcast_to(tiled_pack[None], (owners, lane_rows, 128))
    query_grad, key_grad, spread = lax.optimization_barrier((query_grad, key_grad, spread))
    everyone = lax.all_to_all(spread, "ctx", split_axis=0, concat_axis=0, tiled=True)
    everyone = everyone.reshape(owners, -1)[:, :packed_len].reshape(owners * local_rows, packed.shape[1])
    mode_count = part_residues.shape[1]
    d_residues = everyone[:, :mode_count]
    d_skip = everyone[:, mode_count]
    d_taps = everyone[:, mode_count + 1 :].reshape(-1, part_taps.shape[0], tap_count)
    groups = lax.axis_size("tp")
    here = lax.axis_index("tp")
    rows_each = value_grad.shape[0] // groups
    rolled = jnp.roll(value_grad.reshape(groups, rows_each, -1), -here, axis=0)
    partial_sum = lax.dot_general(
        rolled.reshape(value_grad.shape), w_value, (((1,), (1,)), ((), ())),
        preferred_element_type=jnp.float32,
    )
    narrowed = partial_sum.astype(jnp.bfloat16).reshape(groups, rows_each, -1)
    total = narrowed[0].astype(jnp.float32)
    for shift in range(1, groups):
        incoming = lax.ppermute(
            narrowed[shift], "tp", [(i, (i + shift) % groups) for i in range(groups)]
        )
        total = total + incoming.astype(jnp.float32)
    input_grad = total.astype(jnp.bfloat16)
    return (input_grad, query_grad, key_grad, d_residues, d_skip, d_taps)


def solution(mesh):
    in_specs = (
        P("ctx", "tp"),
        P("ctx", "tp"),
        P("ctx", "tp"),
        P("ctx", "tp"),
        P(None, "tp"),
        P("tp", None, None),
        P("tp", None),
        P("tp", None),
        P("tp"),
    )
    out_specs = (
        P(("ctx", "tp"), None),
        P("ctx", "tp"),
        P("ctx", "tp"),
        P("tp", None),
        P("tp"),
        P("tp", None, None),
    )
    return jax.shard_map(
        on_device, mesh=mesh, in_specs=in_specs, out_specs=out_specs, check_vma=False
    )
```
